128 devices in a mesh: grp: 4 (over y), blk: 32 (over z, x, core).
Axes of the slice: x: 4, y: 4, z: 4, core: 2. Of those that a mesh axis runs over, the one named last changes fastest.
Arguments:
- displacement: float32 [3, 125, 131072], P(None, None, ('grp', 'blk')), may hold values from -0.4 to 0.4, as said below
- velocity: float32 [3, 125, 131072], P(None, None, ('grp', 'blk')), may hold values from -4 to 4, as said below
- lame: float32 [2, 131072], P(None, ('grp', 'blk')), may hold values from 0.5 to 2
- fault_props: float32 [7, 25, 16384], P(None, None, ('grp', 'blk')), may hold values from -4 to 6, as said below
- fault_slots: int32 [16384], P(('grp', 'blk')), may hold values from 0 to 127, as said below
Outputs:
- velocity_new: float32 [3, 125, 131072], P(None, None, ('grp', 'blk'))
- slip_rate: float32 [25, 16384], P(None, ('grp', 'blk'))
- theta_new: float32 [25, 16384], P(None, ('grp', 'blk'))
The draws below stay inside these ranges and needn't reach their ends.
Inputs may be any that keep to these rules, and one draw needn't show every extreme that they name: `fault_slots`: each device's 128 entries are a permutation of 0 to 127. `displacement`: entries at one node shared by several elements are equal, except across the fault plane. `velocity`: entries at one node shared by several elements are equal, except across the fault plane. `fault_props`: Rows: state in 0.3 to 3, a in 0.3 to 0.6, b in 0.1 to 0.4, slip distance in 0.5 to 1.5, two prestresses in -4 to 4, normal stress in 2 to 6; entries of one fault node shared by neighbouring faces are equal.
All inputs are finite; a program needn't handle non-finite values.
Results may differ from the reference program's by a relative error of at most 0.0001.
Values sent between devices are 32-bit elements; how exact they have to be, the bound alone decides.
No kernel may reach another device: no remote copies, remote signals or barrier semaphores. Data moves between devices by JAX's collectives and lax.ppermute only.
A program may use at most 64 MiB of HBM per device.

```python
import math
import jax
import jax.numpy as jnp
import numpy as np
from jax import lax

EX = 4
EY = 8
EZ = 32
NEWTON = 3
NXE = 128
NYE = 8
NZE = 128
NE_ALL = 131072
FAULT = 16384
FDEV = 128
PXF = 32
PZF = 1
PZW = 4
N_GRP = 4
N_BLK = 32
DEVICES = 128


def slot_map(key):
    keys = jax.random.split(jax.random.fold_in(key, 101), DEVICES)
    perms = jax.vmap(lambda single: jax.random.permutation(single, FDEV))(keys)
    return perms.reshape(FAULT).astype(jnp.int32)


def node_field(key, spread):
    grid_x = 4 * NXE + 1
    grid_y = 4 * NYE + 2
    grid_z = 4 * NZE + 1
    shape_all = (5, 5, 5, N_GRP, N_BLK, EX, EY, EZ)
    node_p = lax.broadcasted_iota(jnp.int32, shape_all, 0)
    node_q = lax.broadcasted_iota(jnp.int32, shape_all, 1)
    node_r = lax.broadcasted_iota(jnp.int32, shape_all, 2)
    grp_pos = lax.broadcasted_iota(jnp.int32, shape_all, 3)
    blk_pos = lax.broadcasted_iota(jnp.int32, shape_all, 4)
    elem_i = lax.broadcasted_iota(jnp.int32, shape_all, 5)
    elem_j = lax.broadcasted_iota(jnp.int32, shape_all, 6)
    elem_k = lax.broadcasted_iota(jnp.int32, shape_all, 7)
    glob_x = 4 * (blk_pos * EX + elem_i) + node_p
    glob_y = 4 * elem_j + node_q + (elem_j >= NYE // 2).astype(jnp.int32)
    glob_z = 4 * (grp_pos * EZ + elem_k) + node_r
    flat_index = ((glob_x * grid_y + glob_y) * grid_z + glob_z).reshape(125, NE_ALL)
    node_count = grid_x * grid_y * grid_z
    values = jnp.clip(jax.random.normal(key, (3, node_count), jnp.float32), -4.0, 4.0)
    return spread * jnp.take(values, flat_index, axis=1)


def draw_displacement(key, part):
    return node_field(jax.random.fold_in(key, 1), 0.1)


def draw_velocity(key, part):
    return node_field(jax.random.fold_in(key, 2), 1.0)


def draw_fault_slots(key, part):
    return slot_map(key)


def draw_fault_props(key, part):
    slots = slot_map(key)
    slot_pos = jnp.arange(FAULT, dtype=jnp.int32)
    device = slot_pos // FDEV
    inner_z = slots % PZW
    pos_x = device // N_BLK * PXF + slots // PZW
    pos_z = inner_z // PZF * EZ + device % N_BLK * PZF + inner_z % PZF
    node_p = jnp.arange(25, dtype=jnp.int32)[:, None] // 5
    node_r = jnp.arange(25, dtype=jnp.int32)[:, None] % 5
    flat_index = (4 * pos_x[None] + node_p) * (4 * NZE + 1) + 4 * pos_z[None] + node_r
    node_count = (4 * NXE + 1) * (4 * NZE + 1)
    ranges = [(0.3, 3.0), (0.3, 0.6), (0.1, 0.4), (0.5, 1.5)]
    grids = []
    for number, bounds in enumerate(ranges):
        sample = jax.random.uniform(jax.random.fold_in(key, 200 + number), (node_count,), jnp.float32, jnp.log(bounds[0]), jnp.log(bounds[1]))
        grids.append(jnp.exp(sample))
    for number in range(2):
        sub_key = jax.random.fold_in(key, 300 + number)
        grids.append(jnp.clip(jax.random.normal(sub_key, (node_count,), jnp.float32), -4.0, 4.0))
    grids.append(jax.random.uniform(jax.random.fold_in(key, 400), (node_count,), jnp.float32, 2.0, 6.0))
    stacked = jnp.stack(grids)
    return jnp.take(stacked, flat_index, axis=1)


def block_scale(own_key, shape, pieces, low, high):
    loudness, own = 1.0, jax.random.fold_in(own_key, 6)
    for axis_at, parts in pieces:
        steps = jnp.exp(jax.random.uniform(jax.random.fold_in(own, axis_at), (parts,), jnp.float32, low / len(pieces), high / len(pieces)))
        loudness = loudness * jnp.repeat(steps, shape[axis_at] // parts).reshape([-1 if axis == axis_at else 1 for axis in range(len(shape))])
    return loudness


def setup_inputs(seed: int = 0) -> dict:
    key_list = jax.random.split(jax.random.key(seed), 6)
    displacement = draw_displacement(jax.random.fold_in(key_list[5], 71), 0)
    velocity = draw_velocity(jax.random.fold_in(key_list[5], 71), 0)
    lame = jnp.clip(jnp.exp(math.log(2.0) - 1.3862944 * jax.random.uniform(key_list[2], (2, NE_ALL), jnp.float32) ** block_scale(key_list[2], (2, NE_ALL), ((1, 128),), -0.2, 0.2)), 0.5, 2.0)
    fault_props = draw_fault_props(jax.random.fold_in(key_list[5], 71), 0)
    fault_slots = draw_fault_slots(jax.random.fold_in(key_list[5], 71), 0)
    return dict(displacement=displacement, velocity=velocity, lame=lame, fault_props=fault_props, fault_slots=fault_slots)


GLL_POINTS = np.array([-1.0, -np.sqrt(3.0 / 7.0), 0.0, np.sqrt(3.0 / 7.0), 1.0])
GLL_WEIGHTS = np.array([0.1, 49.0 / 90.0, 32.0 / 45.0, 49.0 / 90.0, 0.1])
DT = 0.01
W_END = 0.1
ETA = W_END / (2.0 * DT)
CORRECTION = DT / W_END
FRICTION_REF = 0.6
TRACTION_FLOOR = 1.0

def derivative_table():
    points = GLL_POINTS
    barycentric = np.array([1.0 / np.prod([points[col_idx] - points[other] for other in range(5) if other != col_idx]) for col_idx in range(5)])
    result_table = np.zeros((5, 5))
    for row_idx in range(5):
        for col_idx in range(5):
            if row_idx != col_idx:
                result_table[row_idx, col_idx] = barycentric[col_idx] / barycentric[row_idx] / (points[row_idx] - points[col_idx])
        result_table[row_idx, row_idx] = -np.sum(result_table[row_idx])
    return result_table

def element_force(displacement, lame):
    derivative = jnp.asarray(derivative_table(), jnp.float32)
    weights = jnp.asarray(GLL_WEIGHTS, jnp.float32)
    highest = lax.Precision.HIGHEST
    grad_x = jnp.einsum('pa,iabce->ipbce', derivative, displacement, precision=highest)
    grad_y = jnp.einsum('qb,iabce->iaqce', derivative, displacement, precision=highest)
    grad_z = jnp.einsum('rc,iabce->iabre', derivative, displacement, precision=highest)
    gradient = jnp.stack([grad_x, grad_y, grad_z])
    dilation = grad_x[0] + grad_y[1] + grad_z[2]
    identity = jnp.eye(3, dtype=jnp.float32)
    stress = lame[0] * dilation * identity[:, :, None, None, None, None] + lame[1] * (gradient + jnp.swapaxes(gradient, 0, 1))
    volume_weight = weights[:, None, None] * weights[None, :, None] * weights[None, None, :]
    weighted = stress * volume_weight[:, :, :, None]
    part_x = jnp.einsum('pa,ipbce->iabce', derivative, weighted[0], precision=highest)
    part_y = jnp.einsum('qb,iaqce->iabce', derivative, weighted[1], precision=highest)
    part_z = jnp.einsum('rc,iabre->iabce', derivative, weighted[2], precision=highest)
    return -(part_x + part_y + part_z)

def pair_sum(field, node_axis, elem_axis, keep_pair):
    reordered = jnp.moveaxis(field, (node_axis, elem_axis), (0, 1))
    upper_face = reordered[4, :-1]
    lower_face = reordered[0, 1:]
    keep_pair = keep_pair.reshape(keep_pair.shape + (1,) * (upper_face.ndim - 1))
    reordered = reordered.at[4, :-1].add(keep_pair * lower_face)
    reordered = reordered.at[0, 1:].add(keep_pair * upper_face)
    return jnp.moveaxis(reordered, (0, 1), (node_axis, elem_axis))

def inverse_sinh(value):
    return jnp.log(value + jnp.sqrt(1.0 + value * value))

def friction(minus_side, plus_side, props):
    theta_old = props[0]
    direct_a = props[1]
    evolve_b = props[2]
    slip_length = props[3]
    prestress_x = props[4]
    prestress_z = props[5]
    normal_stress = props[6]
    slip_jump = plus_side - minus_side
    trial_x = prestress_x + ETA * slip_jump[0]
    trial_z = prestress_z + ETA * slip_jump[2]
    trial_norm = jnp.sqrt(trial_x * trial_x + trial_z * trial_z)
    scale_c = 0.5 * jnp.exp((FRICTION_REF + evolve_b * jnp.log(theta_old / slip_length)) / direct_a)
    slip_rate = jnp.zeros_like(trial_norm)
    for newton_step in range(NEWTON):
        argument = scale_c * slip_rate
        residual = trial_norm - ETA * slip_rate - normal_stress * direct_a * inverse_sinh(argument)
        slope_newton = -ETA - normal_stress * direct_a * scale_c / jnp.sqrt(1.0 + argument * argument)
        slip_rate = slip_rate - residual / slope_newton
    ratio_keep = 1.0 - ETA * slip_rate / jnp.maximum(trial_norm, TRACTION_FLOOR)
    push_back = jnp.stack([trial_x * ratio_keep - prestress_x, ETA * slip_jump[1], trial_z * ratio_keep - prestress_z])
    theta_new = theta_old + DT * (1.0 - slip_rate * theta_old / slip_length)
    return (slip_rate, theta_new, push_back)

def to_grid(field):
    channels = field.shape[0]
    shaped = field.reshape(channels, 5, 5, 5, N_GRP, N_BLK, EX, EY, EZ)
    shaped = jnp.transpose(shaped, (0, 1, 2, 3, 5, 6, 7, 4, 8))
    return shaped.reshape(channels, 5, 5, 5, NXE, NYE, NZE)

def from_grid(field):
    channels = field.shape[0]
    shaped = field.reshape(channels, 5, 5, 5, N_BLK, EX, EY, N_GRP, EZ)
    shaped = jnp.transpose(shaped, (0, 1, 2, 3, 7, 4, 5, 6, 8))
    return shaped.reshape(channels, 125, NE_ALL)

def assemble(field):
    field = pair_sum(field, 3, 6, jnp.ones((NZE - 1,), jnp.float32))
    field = pair_sum(field, 1, 4, jnp.ones((NXE - 1,), jnp.float32))
    keep_rows = jnp.ones((NYE - 1,), jnp.float32).at[NYE // 2 - 1].set(0.0)
    return pair_sum(field, 2, 5, keep_rows)

def reference(displacement, velocity, lame, fault_props, fault_slots):
    device_count = N_GRP * N_BLK
    per_device = EX * EY * EZ
    disp_blocks = jnp.moveaxis(displacement.reshape(3, 5, 5, 5, device_count, per_device), 4, 0)
    lame_blocks = jnp.moveaxis(lame.reshape(2, device_count, per_device), 1, 0)
    forces = lax.map(lambda block_pair: element_force(block_pair[0], block_pair[1]), (disp_blocks, lame_blocks))
    forces = jnp.moveaxis(forces, 0, 4).reshape(3, 5, 5, 5, NE_ALL)
    forces = assemble(to_grid(forces))
    weights = jnp.asarray(GLL_WEIGHTS, jnp.float32)
    volume_weight = weights[:, None, None] * weights[None, :, None] * weights[None, None, :]
    node_mass = assemble(jnp.broadcast_to(volume_weight[None, :, :, :, None, None, None], (1, 5, 5, 5, NXE, NYE, NZE)))
    predicted = to_grid(velocity.reshape(3, 5, 5, 5, NE_ALL)) + DT * forces / node_mass
    slot_pos = jnp.arange(FAULT, dtype=jnp.int32)
    device = slot_pos // FDEV
    inner_z = fault_slots % PZW
    pos_x = device // N_BLK * PXF + fault_slots // PZW
    pos_z = inner_z // PZF * EZ + device % N_BLK * PZF + inner_z % PZF
    flat_index = (pos_x * NZE + pos_z).astype(jnp.int32)
    minus_layer = predicted[:, :, 4, :, :, NYE // 2 - 1, :].reshape(75, NXE * NZE)
    plus_layer = predicted[:, :, 0, :, :, NYE // 2, :].reshape(75, NXE * NZE)
    minus_side = jnp.take(minus_layer, flat_index, axis=1).reshape(3, 25, FAULT)
    plus_side = jnp.take(plus_layer, flat_index, axis=1).reshape(3, 25, FAULT)
    slip_rate, theta_new, push_back = friction(minus_side, plus_side, fault_props)
    push_layer = jnp.zeros((75, NXE * NZE), jnp.float32).at[:, flat_index].set(push_back.reshape(75, FAULT))
    push_layer = push_layer.reshape(3, 5, 5, NXE, NZE)
    predicted = predicted.at[:, :, 4, :, :, NYE // 2 - 1, :].add(CORRECTION * push_layer)
    predicted = predicted.at[:, :, 0, :, :, NYE // 2, :].add(-CORRECTION * push_layer)
    return (from_grid(predicted), slip_rate, theta_new)
```

```python
import jax
import jax.numpy as jnp
import numpy as np
from jax import lax
from jax.experimental import pallas as pl
from jax.experimental.pallas import tpu as pltpu
from jax.sharding import PartitionSpec as P

NEWTON = 3
GLL_POINTS = np.array([-1.0, -np.sqrt(3.0 / 7.0), 0.0, np.sqrt(3.0 / 7.0), 1.0])
GLL_WEIGHTS = np.array([0.1, 49.0 / 90.0, 32.0 / 45.0, 49.0 / 90.0, 0.1])
DT = 0.01
W_END = 0.1
ETA = W_END / (2.0 * DT)
CORRECTION = DT / W_END
FRICTION_REF = 0.6
TRACTION_FLOOR = 1.0
N_GRP = 4
N_BLK = 32
F32 = jnp.float32
HIGHEST = lax.Precision.HIGHEST


def derivative_table():
    x = GLL_POINTS
    bary = [1.0 / np.prod([x[c] - x[o] for o in range(5) if o != c]) for c in range(5)]
    table = np.zeros((5, 5))
    for r in range(5):
        for c in range(5):
            if r != c:
                table[r, c] = bary[c] / bary[r] / (x[r] - x[c])
        table[r, r] = -np.sum(table[r])
    return table


D_TABLE = derivative_table()
M_TABLE = -DT * D_TABLE.T * GLL_WEIGHTS[None, :] / GLL_WEIGHTS[:, None]


def line(table, u):
    e0, e1 = u[0] + u[4], u[1] + u[3]
    o0, o1 = u[0] - u[4], u[1] - u[3]
    out = [None] * 5
    for i in range(2):
        even = (
            float((table[i, 0] + table[i, 4]) / 2) * e0
            + float((table[i, 1] + table[i, 3]) / 2) * e1
            + float(table[i, 2]) * u[2]
        )
        odd = (
            float((table[i, 0] - table[i, 4]) / 2) * o0
            + float((table[i, 1] - table[i, 3]) / 2) * o1
        )
        out[i] = odd + even
        out[4 - i] = odd - even
    out[2] = float(table[2, 0]) * o0 + float(table[2, 1]) * o1
    return out


def node(p, q, r):
    return 25 * p + 5 * q + r


def roll(x, shift, axis):
    shift = shift % x.shape[axis]
    return x if shift == 0 else pltpu.roll(x, shift, axis)


def row(ref, c, n):
    return ref[c, n, :].reshape(8, 128)


def tile_iota():
    lane = lax.broadcasted_iota(jnp.int32, (8, 128), 1)
    sub = lax.broadcasted_iota(jnp.int32, (8, 128), 0)
    return lane, sub, lane // 32, lane % 32, sub // 2


def inverse_sinh(value):
    return jnp.log(value + jnp.sqrt(1.0 + value * value))


def own_scales(grp, blk):
    half = lambda has: jnp.where(has, 0.5, 1.0).astype(F32)
    return half(blk > 0), half(blk < N_BLK - 1), half(grp > 0), half(grp < N_GRP - 1)


def slot_hot(slots):
    r = lax.broadcasted_iota(jnp.int32, (128, 128), 0)
    face = (r % 8) * 16 + (r // 8 % 4) * 4 + r // 32
    return (jnp.broadcast_to(slots, (128, 128)) == face).astype(F32)


def fault_jump(get):
    return get(0) - roll(roll(get(4), 32, 1), 1, 0)


def force_kernel(
    disp, vel, lame, props, slots,
    f_out, xe_out, xo_out, ze_out, zo_out, abuf,
    gx, gy, sj, xs, sc,
):
    grp = lax.axis_index("grp")
    blk = lax.axis_index("blk")
    lane, sub, jl, k, i_el = tile_iota()
    lam = lame[0, :].reshape(8, 128)
    mu = lame[1, :].reshape(8, 128)
    mu2 = mu + mu
    x0, x4, z0, z4 = own_scales(grp, blk)

    for c in range(3):
        for r in range(5):
            u = [[row(disp, c, node(p, q, r)) for q in range(5)] for p in range(5)]
            for q in range(5):
                out = line(D_TABLE, [u[p][q] for p in range(5)])
                for p in range(5):
                    gx[c, node(p, q, r)] = out[p]
            for p in range(5):
                out = line(D_TABLE, u[p])
                for q in range(5):
                    gy[c, node(p, q, r)] = out[q]

    for p in range(5):
        for q in range(5):
            gz = [
                line(D_TABLE, [row(disp, c, node(p, q, r)) for r in range(5)]) for c in range(3)
            ]
            sz = [[None] * 5 for _ in range(3)]
            for r in range(5):
                n = node(p, q, r)
                g0 = [gx[c, n] for c in range(3)]
                g1 = [gy[c, n] for c in range(3)]
                g2 = [gz[c][r] for c in range(3)]
                spread = lam * (g0[0] + g1[1] + g2[2])
                s01 = mu * (g0[1] + g1[0])
                s02 = mu * (g0[2] + g2[0])
                s12 = mu * (g1[2] + g2[1])
                gx[0, n] = spread + mu2 * g0[0]
                gx[1, n] = s01
                gx[2, n] = s02
                gy[1, n] = spread + mu2 * g1[1]
                gy[2, n] = s12
                sz[0][r], sz[1][r], sz[2][r] = s02, s12, spread + mu2 * g2[2]
            for c in range(3):
                out = line(M_TABLE, sz[c])
                for r in range(5):
                    f_out[c, node(p, q, r)] = out[r]

    y4_in, y0_in = jl < 3, jl > 0
    x4_in, x0_in = i_el < 3, i_el > 0
    for c in range(3):
        for r in range(5):
            f = [[f_out[c, node(p, q, r)] for q in range(5)] for p in range(5)]
            for p in range(5):
                if c == 0:
                    s = [gx[1, node(p, q, r)] for q in range(5)]
                else:
                    s = [gy[c, node(p, q, r)] for q in range(5)]
                out = line(M_TABLE, s)
                for q in range(5):
                    f[p][q] = f[p][q] + out[q]
            for q in range(5):
                out = line(M_TABLE, [gx[c, node(p, q, r)] for p in range(5)])
                for p in range(5):
                    f[p][q] = f[p][q] + out[p]
            for p in range(5):
                avg = 0.5 * (f[p][4] + roll(f[p][0], -32, 1))
                f[p][0] = jnp.where(y0_in, roll(avg, 32, 1), f[p][0])
                f[p][4] = jnp.where(y4_in, avg, f[p][4])
            for q in range(5):
                avg = 0.5 * (f[4][q] + roll(f[0][q], -2, 0))
                f[0][q] = jnp.where(x0_in, roll(avg, 2, 0), f[0][q] * x0)
                f[4][q] = jnp.where(x4_in, avg, f[4][q] * x4)
            for p in range(5):
                for q in range(5):
                    f_out[c, node(p, q, r)] = f[p][q]

    z4_in, z0_in = k < 31, k > 0
    zero = jnp.zeros((8, 128), F32)
    zlo, zhi = [zero] * 3, [zero] * 3
    for c in range(3):
        for p in range(5):
            for q in range(5):
                n0, n4 = node(p, q, 0), node(p, q, 4)
                a0, a4 = f_out[c, n0], f_out[c, n4]
                avg = 0.5 * (a4 + roll(a0, -1, 1))
                a0 = jnp.where(z0_in, roll(avg, 1, 1), a0 * z0)
                a4 = jnp.where(z4_in, avg, a4 * z4)
                f_out[c, n0] = a0
                f_out[c, n4] = a4
                m = c * 25 + p * 5 + q
                at = k == m % 32
                zlo[m // 32] = jnp.where(at, roll(a0, m % 32, 1), zlo[m // 32])
                zhi[m // 32] = jnp.where(at, roll(a4, m % 32 - 31, 1), zhi[m // 32])
    z_even = grp % 2 == 0
    for g in range(3):
        ze_out[g] = jnp.where(z_even, zhi[g], zlo[g])
        zo_out[g] = jnp.where(z_even, zlo[g], zhi[g])

    x_even = blk % 2 == 0
    for c in range(3):
        for q in range(5):
            for r in range(5):
                m = c * 25 + q * 5 + r
                lo = f_out[c, node(0, q, r)]
                hi = roll(f_out[c, node(4, q, r)], 2, 0)
                xe_out[m] = jnp.where(x_even, hi, lo)[0:2]
                xo_out[m] = jnp.where(x_even, lo, hi)[0:2]

    for t in range(128):
        abuf[pl.ds(8 * t, 8), :] = zero
    own_x = {0: jnp.where(x0_in, 1.0, x0), 4: jnp.where(x4_in, 1.0, x4)}
    own_z = {0: jnp.where(z0_in, 1.0, z0), 4: jnp.where(z4_in, 1.0, z4)}
    for p in range(5):
        for c in range(3):
            jump = [None] * 5
            for r in range(5):
                own = None
                for part in (own_x.get(p), own_z.get(r)):
                    if part is not None:
                        own = part if own is None else own * part

                def side(q, own=own, r=r):
                    v = row(vel, c, node(p, q, r))
                    return f_out[c, node(p, q, r)] + (v if own is None else v * own)

                jump[r] = fault_jump(side)
                sj[pl.ds(8 * (p * 24 + c * 8 + r), 8), :] = jump[r]
            extra = jnp.where(k == 0, roll(jump[4], -31, 1), 0.0)
            extra = jnp.where(k == 31, roll(jump[0], 31, 1), extra)
            sj[pl.ds(8 * (p * 24 + c * 8 + 5), 8), :] = extra
            sj[pl.ds(8 * (p * 24 + c * 8 + 6), 8), :] = zero
            sj[pl.ds(8 * (p * 24 + c * 8 + 7), 8), :] = zero
    for t in range(120, 128):
        sj[pl.ds(8 * t, 8), :] = zero
    lane_big = lax.broadcasted_iota(jnp.int32, (128, 128), 1)
    y = None
    for i in range(4):
        part = roll(sj[pl.ds(2 * i + 1, 128, stride=8), :], 32 * i, 1)
        y = part if y is None else jnp.where(lane_big // 32 == i, part, y)
    yt = y.T
    dest = blk // 8

    def put_jump(d):
        for i in range(4):
            abuf[pl.ds(d * 256 + i, 32, stride=8), :] = yt[32 * i : 32 * i + 32]

    put_jump(dest)

    @pl.when((blk % 8 == 7) & (dest < N_GRP - 1))
    def _():
        put_jump(dest + 1)

    @pl.when((blk % 8 == 0) & (dest > 0))
    def _():
        put_jump(dest - 1)

    xs[...] = jnp.zeros((128, 128), F32)
    theta, a, b, length = props[0], props[1], props[2], props[3]
    xs[0:25] = props[4]
    xs[32:57] = props[5]
    xs[64:89] = 0.5 * jnp.exp((FRICTION_REF + b * jnp.log(theta / length)) / a)
    xs[96:121] = props[6] * a
    packed = lax.dot_general(
        slot_hot(slots[...]), xs[...], (((1,), (1,)), ((), ())),
        precision=HIGHEST, preferred_element_type=F32,
    )
    for u in range(4):
        for i in range(4):
            t = u * 4 + i
            abuf[pl.ds(u * 256 + grp * 64 + 4 + i, 8, stride=8), :] = packed[8 * t : 8 * t + 8]

    sc[pl.ds(120, 8), :] = zero
    for q in range(5):
        for c in range(3):
            low = jnp.where(k < 16, f_out[c, node(0, q, 0)], f_out[c, node(0, q, 4)])
            high = jnp.where(k < 16, f_out[c, node(4, q, 0)], f_out[c, node(4, q, 4)])
            sc[pl.ds(q * 24 + c * 8, 8), :] = jnp.where(sub < 4, low, high)
    sc[...] = sc[...].T
    at_edge = lax.broadcasted_iota(jnp.int32, (4, 128), 1) % 8 >= 6
    for dg in (-1, 1):
        for db in (-1, 1):
            ok = (grp + dg >= 0) & (grp + dg < N_GRP) & (blk + db >= 0) & (blk + db < N_BLK)
            value = sc[pl.ds(31 if dg > 0 else 0, 4, stride=32), :]
            if db < 0:
                value = roll(value, 6, 1)

            @pl.when(ok)
            def _(value=value, dg=dg, db=db):
                at = 8 * ((grp + dg) * N_BLK + blk + db)
                abuf[pl.ds(at, 4), :] = jnp.where(at_edge, value, abuf[pl.ds(at, 4), :])


def solve(trial_x, trial_z, scale_c, sigma_a):
    trial_norm = jnp.sqrt(trial_x * trial_x + trial_z * trial_z)
    rate = jnp.zeros_like(trial_norm)
    for _ in range(NEWTON):
        arg = scale_c * rate
        residual = trial_norm - ETA * rate - sigma_a * inverse_sinh(arg)
        slope = -ETA - sigma_a * scale_c / jnp.sqrt(1.0 + arg * arg)
        rate = rate - residual / slope
    return trial_norm, rate


def final_kernel(
    f_in, vel, xe, xo, ze, zo, ain, props, slots,
    v_out, rate_out, theta_out,
    pr, sj, sb, xs, ys, jp,
):
    grp = lax.axis_index("grp")
    blk = lax.axis_index("blk")
    lane, sub, jl, k, i_el = tile_iota()
    zero = jnp.zeros((8, 128), F32)
    lane_big = lax.broadcasted_iota(jnp.int32, (128, 128), 1)

    for c in range(3):
        for n in range(125):
            pr[c, n] = f_in[c, n] + row(vel, c, n)
    x_even = blk % 2 == 0
    for c in range(3):
        for q in range(5):
            for r in range(5):
                m = c * 25 + q * 5 + r
                ev, od = xe[m], xo[m]
                lo, hi = node(0, q, r), node(4, q, r)
                pr[c, lo, 0:2] = pr[c, lo, 0:2] + jnp.where(x_even, od, ev)
                pr[c, hi, 6:8] = pr[c, hi, 6:8] + jnp.where(x_even, ev, od)
    z_even = grp % 2 == 0
    zlo = [jnp.where(z_even, zo[g], ze[g]) for g in range(3)]
    zhi = [jnp.where(z_even, ze[g], zo[g]) for g in range(3)]

    xs[...] = jnp.zeros((128, 128), F32)
    slot4 = lax.broadcasted_iota(jnp.int32, (4, 128), 1) % 8
    for dg in (-1, 1):
        value = None
        for db in (-1, 1):
            ok = (grp + dg >= 0) & (grp + dg < N_GRP) & (blk + db >= 0) & (blk + db < N_BLK)
            at = jnp.where(ok, 8 * ((grp + dg) * N_BLK + blk + db), 0)
            part = ain[pl.ds(pl.multiple_of(at, 8), 4), :]
            part = jnp.where((slot4 >= 6) & ok, part, 0.0)
            value = roll(part, -6, 1) if value is None else value + part
        xs[pl.ds(31 if dg > 0 else 0, 4, stride=32), :] = value
    edges = xs[...].T
    for c in range(3):
        for p in range(5):
            for q in range(5):
                m = c * 25 + p * 5 + q
                n0, n4 = node(p, q, 0), node(p, q, 4)
                add0 = roll(zlo[m // 32], -(m % 32), 1)
                add4 = roll(zhi[m // 32], 31 - m % 32, 1)
                if p in (0, 4):
                    edge = edges[q * 24 + c * 8 : q * 24 + c * 8 + 8]
                    edge = jnp.where((sub < 4) == (p == 0), edge, 0.0)
                    add0, add4 = add0 + edge, add4 + edge
                pr[c, n0] = pr[c, n0] + jnp.where(k == 0, add0, 0.0)
                pr[c, n4] = pr[c, n4] + jnp.where(k == 31, add4, 0.0)

    for c in range(3):
        for p in range(5):
            for r in range(5):
                sj[pl.ds(8 * (c * 32 + p * 5 + r), 8), :] = fault_jump(
                    lambda q: pr[c, node(p, q, r)]
                )
    lane96 = lax.broadcasted_iota(jnp.int32, (96, 128), 1) // 32
    jump = None
    for i in range(4):
        part = roll(sj[pl.ds(2 * i + 1, 96, stride=8), :], 32 * i, 1)
        jump = part if jump is None else jnp.where(lane96 == i, part, jump)
    for i in range(4):
        ys[pl.ds(32 * i, 32), :] = ain[pl.ds(blk // 8 * 256 + 4 + i, 32, stride=8), :]
    par = ys[...].T
    t0x, t0z, scale_c, sigma_a = par[0:32], par[32:64], par[64:96], par[96:128]
    trial_x = t0x + ETA * jump[0:32]
    trial_z = t0z + ETA * jump[64:96]
    trial_norm, rate = solve(trial_x, trial_z, scale_c, sigma_a)
    keep = 1.0 - ETA * rate / jnp.maximum(trial_norm, TRACTION_FLOOR)
    push = (
        CORRECTION * (trial_x * keep - t0x),
        CORRECTION * ETA * jump[32:64],
        CORRECTION * (trial_z * keep - t0z),
    )
    for c in range(3):
        for i in range(4):
            sb[pl.ds(c * 256 + 2 * i + 1, 32, stride=8), :] = roll(push[c], -32 * i, 1)
            sb[pl.ds(c * 256 + 2 * i, 32, stride=8), :] = roll(push[c], 96 - 32 * i, 1)
    plus_at = (sub % 2 == 1) & (lane < 32)
    minus_at = (sub % 2 == 0) & (lane >= 96)
    for c in range(3):
        for p in range(5):
            for r in range(5):
                n0, n4 = node(p, 0, r), node(p, 4, r)
                push_back = sb[pl.ds(8 * (c * 32 + p * 5 + r), 8), :]
                pr[c, n0] = pr[c, n0] - jnp.where(plus_at, push_back, 0.0)
                pr[c, n4] = pr[c, n4] + jnp.where(minus_at, push_back, 0.0)
    for c in range(3):
        for n in range(125):
            v_out[c, n, :] = pr[c, n].reshape(1024)

    for u in range(4):
        for i in range(4):
            ys[pl.ds(8 * (u * 4 + i), 8), :] = ain[
                pl.ds(u * 256 + grp * 64 + i, 8, stride=8), :
            ]
    xs[...] = jnp.zeros((128, 128), F32)
    for u in range(4):
        for step, there, at, into in ((-1, grp > 0, 3, 0), (8, grp < N_GRP - 1, 0, 31)):
            source = jnp.where(there, (u * 32 + grp * 8 + step) * 8 + at, 0)
            value = ain[pl.ds(source, 1), :]
            xs[pl.ds(u * 32 + into, 1), :] = jnp.where(there, value, 0.0)
    body, ends = ys[...].T, xs[...].T
    first = jnp.where(grp_is(blk, 0), 1.0, 0.0).astype(F32)
    last = jnp.where(grp_is(blk, N_BLK - 1), 1.0, 0.0).astype(F32)

    def along_z(mat, p, c):
        at = p * 24 + c * 8
        t = mat[at : at + 8]
        low = jnp.where((sub == 0) & (lane >= 32), roll(roll(t, 32, 1), -5, 0), 0.0)
        high = jnp.where((sub == 4) & (lane < 96), roll(roll(t, -32, 1), -1, 0), 0.0)
        return t + low * first + high * last

    i_at, s_at = lane // 8 % 4, lane % 8
    for c in (0, 2):
        t = [along_z(body, p, c) for p in range(5)]
        end0, end4 = along_z(ends, 0, c), along_z(ends, 4, c)
        left = jnp.where(s_at == 0, end4, roll(t[4], -23, 1))
        right = jnp.where(s_at == 7, end0, roll(t[0], 23, 1))
        t[0], t[4] = (
            t[0] + jnp.where(i_at == 0, left, 0.0),
            t[4] + jnp.where(i_at == 3, right, 0.0),
        )
        for p in range(5):
            jp[c // 2, 5 * p : 5 * p + 5, :] = t[p][0:5]
    hot = slot_hot(slots[...])
    slot_jump = [
        lax.dot_general(
            jp[c], hot, (((1,), (0,)), ((), ())), precision=HIGHEST, preferred_element_type=F32
        )[0:25]
        for c in range(2)
    ]
    theta, a, b, length = props[0], props[1], props[2], props[3]
    scale_c = 0.5 * jnp.exp((FRICTION_REF + b * jnp.log(theta / length)) / a)
    _, rate = solve(
        props[4] + ETA * slot_jump[0], props[5] + ETA * slot_jump[1], scale_c, props[6] * a
    )
    rate_out[...] = rate
    theta_out[...] = theta + DT * (1.0 - rate * theta / length)


def grp_is(index, value):
    return index == value


def on_device(displacement, velocity, lame, fault_props, fault_slots):
    slots = fault_slots.reshape(1, 128)
    shape = lambda *s: jax.ShapeDtypeStruct(s, F32)
    vmem = lambda *s: pltpu.VMEM(s, F32)
    f, xe, xo, ze, zo, abuf = pl.pallas_call(
        force_kernel,
        name="force",
        out_shape=(
            shape(3, 125, 8, 128), shape(75, 2, 128), shape(75, 2, 128),
            shape(3, 8, 128), shape(3, 8, 128), shape(1024, 128),
        ),
        scratch_shapes=[
            vmem(3, 125, 8, 128), vmem(3, 125, 8, 128), vmem(1024, 128), vmem(128, 128),
            vmem(128, 128),
        ],
    )(displacement, velocity, lame, fault_props, slots)
    ain = lax.all_to_all(abuf, ("grp", "blk"), 0, 0, tiled=True)
    even_b = [(i, i ^ 1) for i in range(N_BLK)]
    odd_b = [(i, ((i + 1) ^ 1) - 1) for i in range(1, N_BLK - 1)]
    even_g = [(i, i ^ 1) for i in range(N_GRP)]
    odd_g = [(i, ((i + 1) ^ 1) - 1) for i in range(1, N_GRP - 1)]
    xe = lax.ppermute(xe, "blk", even_b)
    xo = lax.ppermute(xo, "blk", odd_b)
    ze = lax.ppermute(ze, "grp", even_g)
    zo = lax.ppermute(zo, "grp", odd_g)
    return pl.pallas_call(
        final_kernel,
        name="final",
        out_shape=(shape(3, 125, 1024), shape(25, 128), shape(25, 128)),
        scratch_shapes=[
            vmem(3, 125, 8, 128), vmem(768, 128), vmem(768, 128), vmem(128, 128),
            vmem(128, 128), vmem(2, 32, 128),
        ],
    )(f, velocity, xe, xo, ze, zo, ain, fault_props, slots)


def solution(mesh):
    both = ("grp", "blk")
    return jax.shard_map(
        on_device,
        mesh=mesh,
        in_specs=(P(None, None, both), P(None, None, both), P(None, both), P(None, None, both), P(both)),
        out_specs=(P(None, None, both), P(None, both), P(None, both)),
        check_vma=False,
    )
```

```python
import jax
import jax.numpy as jnp
import numpy as np
from jax import lax
from jax.experimental import pallas as pl
from jax.experimental.pallas import tpu as pltpu
from jax.sharding import PartitionSpec as P

NEWTON = 3
GLL_POINTS = np.array([-1.0, -np.sqrt(3.0 / 7.0), 0.0, np.sqrt(3.0 / 7.0), 1.0])
GLL_WEIGHTS = np.array([0.1, 49.0 / 90.0, 32.0 / 45.0, 49.0 / 90.0, 0.1])
DT = 0.01
W_END = 0.1
ETA = W_END / (2.0 * DT)
CORRECTION = DT / W_END
FRICTION_REF = 0.6
TRACTION_FLOOR = 1.0
N_GRP = 4
N_BLK = 32
F32 = jnp.float32
HIGHEST = lax.Precision.HIGHEST


def derivative_table():
    x = GLL_POINTS
    bary = [1.0 / np.prod([x[c] - x[o] for o in range(5) if o != c]) for c in range(5)]
    table = np.zeros((5, 5))
    for r in range(5):
        for c in range(5):
            if r != c:
                table[r, c] = bary[c] / bary[r] / (x[r] - x[c])
        table[r, r] = -np.sum(table[r])
    return table


D_TABLE = derivative_table()
M_TABLE = -DT * D_TABLE.T * GLL_WEIGHTS[None, :] / GLL_WEIGHTS[:, None]


def line(table, u):
    e0, e1 = u[0] + u[4], u[1] + u[3]
    o0, o1 = u[0] - u[4], u[1] - u[3]
    out = [None] * 5
    for i in range(2):
        even = (
            float((table[i, 0] + table[i, 4]) / 2) * e0
            + float((table[i, 1] + table[i, 3]) / 2) * e1
            + float(table[i, 2]) * u[2]
        )
        odd = (
            float((table[i, 0] - table[i, 4]) / 2) * o0
            + float((table[i, 1] - table[i, 3]) / 2) * o1
        )
        out[i] = odd + even
        out[4 - i] = odd - even
    out[2] = float(table[2, 0]) * o0 + float(table[2, 1]) * o1
    return out


def node(p, q, r):
    return 25 * p + 5 * q + r


def roll(x, shift, axis):
    shift = shift % x.shape[axis]
    return x if shift == 0 else pltpu.roll(x, shift, axis)


def row(ref, c, n):
    return ref[c, n, :].reshape(8, 128)


def tile_iota():
    lane = lax.broadcasted_iota(jnp.int32, (8, 128), 1)
    sub = lax.broadcasted_iota(jnp.int32, (8, 128), 0)
    return lane, sub, lane // 32, lane % 32, sub // 2


def inverse_sinh(value):
    return jnp.log(value + jnp.sqrt(1.0 + value * value))


def own_scales(grp, blk):
    half = lambda has: jnp.where(has, 0.5, 1.0).astype(F32)
    return half(blk > 0), half(blk < N_BLK - 1), half(grp > 0), half(grp < N_GRP - 1)


def slot_hot(slots):
    r = lax.broadcasted_iota(jnp.int32, (128, 128), 0)
    face = (r % 8) * 16 + (r // 8 % 4) * 4 + r // 32
    return (jnp.broadcast_to(slots, (128, 128)) == face).astype(F32)


def fault_lanes(ref, rows):
    block = lax.broadcasted_iota(jnp.int32, (rows, 128), 1) // 32
    plus = [roll(ref[pl.ds(2 * i + 1, rows, stride=8), :], 32 * i, 1) for i in range(4)]
    minus = [roll(ref[pl.ds(2 * i, rows, stride=8), :], 32 * i - 96, 1) for i in range(4)]
    out = plus[0] - minus[0]
    for i in range(1, 4):
        out = jnp.where(block == i, plus[i] - minus[i], out)
    return out


def force_kernel(
    disp, vel, lame, props, slots,
    f_out, xe_out, xo_out, ze_out, zo_out, abuf,
    gx, gy, sj, xs, sc,
):
    grp = lax.axis_index("grp")
    blk = lax.axis_index("blk")
    lane, sub, jl, k, i_el = tile_iota()
    lam = lame[0, :].reshape(8, 128)
    mu = lame[1, :].reshape(8, 128)
    mu2 = mu + mu
    x0, x4, z0, z4 = own_scales(grp, blk)

    for c in range(3):
        for r in range(5):
            u = [[row(disp, c, node(p, q, r)) for q in range(5)] for p in range(5)]
            for q in range(5):
                out = line(D_TABLE, [u[p][q] for p in range(5)])
                for p in range(5):
                    gx[c, node(p, q, r)] = out[p]
            for p in range(5):
                out = line(D_TABLE, u[p])
                for q in range(5):
                    gy[c, node(p, q, r)] = out[q]

    for p in range(5):
        for q in range(5):
            gz = [
                line(D_TABLE, [row(disp, c, node(p, q, r)) for r in range(5)]) for c in range(3)
            ]
            sz = [[None] * 5 for _ in range(3)]
            for r in range(5):
                n = node(p, q, r)
                g0 = [gx[c, n] for c in range(3)]
                g1 = [gy[c, n] for c in range(3)]
                g2 = [gz[c][r] for c in range(3)]
                spread = lam * (g0[0] + g1[1] + g2[2])
                s01 = mu * (g0[1] + g1[0])
                s02 = mu * (g0[2] + g2[0])
                s12 = mu * (g1[2] + g2[1])
                gx[0, n] = spread + mu2 * g0[0]
                gx[1, n] = s01
                gx[2, n] = s02
                gy[1, n] = spread + mu2 * g1[1]
                gy[2, n] = s12
                sz[0][r], sz[1][r], sz[2][r] = s02, s12, spread + mu2 * g2[2]
            for c in range(3):
                out = line(M_TABLE, sz[c])
                for r in range(5):
                    f_out[c, node(p, q, r)] = out[r]

    y4_in, y0_in = jl < 3, jl > 0
    x4_in, x0_in = i_el < 3, i_el > 0
    z4_in, z0_in = k < 31, k > 0
    zero = jnp.zeros((8, 128), F32)

    def xy_parts(c, r):
        f = [[f_out[c, node(p, q, r)] for q in range(5)] for p in range(5)]
        for p in range(5):
            if c == 0:
                s = [gx[1, node(p, q, r)] for q in range(5)]
            else:
                s = [gy[c, node(p, q, r)] for q in range(5)]
            out = line(M_TABLE, s)
            for q in range(5):
                f[p][q] = f[p][q] + out[q]
        for q in range(5):
            out = line(M_TABLE, [gx[c, node(p, q, r)] for p in range(5)])
            for p in range(5):
                f[p][q] = f[p][q] + out[p]
        for p in range(5):
            up, down = roll(f[p][0], -32, 1), roll(f[p][4], 32, 1)
            f[p][0], f[p][4] = (
                jnp.where(y0_in, 0.5 * (f[p][0] + down), f[p][0]),
                jnp.where(y4_in, 0.5 * (f[p][4] + up), f[p][4]),
            )
        for q in range(5):
            avg = 0.5 * (f[4][q] + roll(f[0][q], -2, 0))
            f[0][q] = jnp.where(x0_in, roll(avg, 2, 0), f[0][q] * x0)
            f[4][q] = jnp.where(x4_in, avg, f[4][q] * x4)
        for p in range(5):
            for q in range(5):
                f_out[c, node(p, q, r)] = f[p][q]

    for c in range(3):
        xy_parts(c, 0)
        xy_parts(c, 4)
        for p in range(5):
            for q in range(5):
                n0, n4 = node(p, q, 0), node(p, q, 4)
                a0, a4 = f_out[c, n0], f_out[c, n4]
                up, down = roll(a0, -1, 1), roll(a4, 1, 1)
                f_out[c, n0] = jnp.where(z0_in, 0.5 * (a0 + down), a0 * z0)
                f_out[c, n4] = jnp.where(z4_in, 0.5 * (a4 + up), a4 * z4)
        for r in (1, 2, 3):
            xy_parts(c, r)

    z_even = grp % 2 == 0
    for g in range(3):
        zlo, zhi = zero, zero
        for m in range(32 * g, min(75, 32 * g + 32)):
            c, pq = m // 25, m % 25
            at = k == m % 32
            zlo = jnp.where(at, roll(f_out[c, 5 * pq], m % 32, 1), zlo)
            zhi = jnp.where(at, roll(f_out[c, 5 * pq + 4], m % 32 - 31, 1), zhi)
        ze_out[g] = jnp.where(z_even, zhi, zlo)
        zo_out[g] = jnp.where(z_even, zlo, zhi)

    x_even = blk % 2 == 0
    for c in range(3):
        for q in range(5):
            for r in range(5):
                m = c * 25 + q * 5 + r
                lo = f_out[c, node(0, q, r)]
                hi = roll(f_out[c, node(4, q, r)], 2, 0)
                xe_out[m] = jnp.where(x_even, hi, lo)[0:2]
                xo_out[m] = jnp.where(x_even, lo, hi)[0:2]

    for t in range(128):
        abuf[pl.ds(8 * t, 8), :] = zero
    own_x = {0: jnp.where(x0_in, 1.0, x0), 4: jnp.where(x4_in, 1.0, x4)}
    own_z = {0: jnp.where(z0_in, 1.0, z0), 4: jnp.where(z4_in, 1.0, z4)}
    odd_sub = sub % 2 == 1
    for p in range(5):
        for cc in range(2):
            c = 2 * cc
            sides = [None] * 5
            for r in range(5):
                own = None
                for part in (own_x.get(p), own_z.get(r)):
                    if part is not None:
                        own = part if own is None else own * part
                n0, n4 = node(p, 0, r), node(p, 4, r)
                v = jnp.where(odd_sub, row(vel, c, n0), row(vel, c, n4))
                f = jnp.where(odd_sub, f_out[c, n0], f_out[c, n4])
                sides[r] = f + (v if own is None else v * own)
                sj[pl.ds(8 * (p * 16 + cc * 8 + r), 8), :] = sides[r]
            extra = jnp.where(k == 0, roll(sides[4], -31, 1), 0.0)
            extra = jnp.where(k == 31, roll(sides[0], 31, 1), extra)
            sj[pl.ds(8 * (p * 16 + cc * 8 + 5), 8), :] = extra
            sj[pl.ds(8 * (p * 16 + cc * 8 + 6), 8), :] = zero
            sj[pl.ds(8 * (p * 16 + cc * 8 + 7), 8), :] = zero
    y = fault_lanes(sj, 80)
    yt = jnp.concatenate([y, jnp.zeros((48, 128), F32)]).T
    dest = blk // 8

    def put_jump(d):
        for i in range(4):
            abuf[pl.ds(d * 256 + i, 32, stride=8), :] = yt[32 * i : 32 * i + 32]

    put_jump(dest)

    @pl.when((blk % 8 == 7) & (dest < N_GRP - 1))
    def _():
        put_jump(dest + 1)

    @pl.when((blk % 8 == 0) & (dest > 0))
    def _():
        put_jump(dest - 1)

    xs[...] = jnp.zeros((128, 128), F32)
    theta, a, b, length, pre_x, pre_z, sigma = (props[:, i, :] for i in range(7))
    xs[0:25] = pre_x
    xs[32:57] = pre_z
    xs[64:89] = 0.5 * jnp.exp((FRICTION_REF + b * jnp.log(theta / length)) / a)
    xs[96:121] = sigma * a
    packed = lax.dot_general(
        slot_hot(slots[...]), xs[...], (((1,), (1,)), ((), ())),
        precision=HIGHEST, preferred_element_type=F32,
    )
    for u in range(4):
        for i in range(4):
            t = u * 4 + i
            abuf[pl.ds(u * 256 + grp * 64 + 4 + i, 8, stride=8), :] = packed[8 * t : 8 * t + 8]

    sc[pl.ds(120, 8), :] = zero
    for q in range(5):
        for c in range(3):
            low = jnp.where(k < 16, f_out[c, node(0, q, 0)], f_out[c, node(0, q, 4)])
            high = jnp.where(k < 16, f_out[c, node(4, q, 0)], f_out[c, node(4, q, 4)])
            sc[pl.ds(q * 24 + c * 8, 8), :] = jnp.where(sub < 4, low, high)
    sc[...] = sc[...].T
    at_edge = lax.broadcasted_iota(jnp.int32, (4, 128), 1) % 8 >= 6
    for dg in (-1, 1):
        for db in (-1, 1):
            ok = (grp + dg >= 0) & (grp + dg < N_GRP) & (blk + db >= 0) & (blk + db < N_BLK)
            value = sc[pl.ds(31 if dg > 0 else 0, 4, stride=32), :]
            if db < 0:
                value = roll(value, 6, 1)

            @pl.when(ok)
            def _(value=value, dg=dg, db=db):
                at = 8 * ((grp + dg) * N_BLK + blk + db)
                abuf[pl.ds(at, 4), :] = jnp.where(at_edge, value, abuf[pl.ds(at, 4), :])


def solve(trial_x, trial_z, scale_c, sigma_a):
    trial_norm = jnp.sqrt(trial_x * trial_x + trial_z * trial_z)
    rate = jnp.zeros_like(trial_norm)
    for _ in range(NEWTON):
        arg = scale_c * rate
        residual = trial_norm - ETA * rate - sigma_a * inverse_sinh(arg)
        slope = -ETA - sigma_a * scale_c / jnp.sqrt(1.0 + arg * arg)
        rate = rate - residual / slope
    return trial_norm, rate


def final_kernel(
    f_in, vel, xe, xo, ze, zo, ain, props, slots,
    v_out, rate_out, theta_out,
    pr, sj, sb, xs, ys, jp,
):
    grp = lax.axis_index("grp")
    blk = lax.axis_index("blk")
    lane, sub, jl, k, i_el = tile_iota()
    zero = jnp.zeros((8, 128), F32)
    lane_big = lax.broadcasted_iota(jnp.int32, (128, 128), 1)

    for c in range(3):
        for n in range(125):
            pr[c, n] = f_in[c, n] + row(vel, c, n)
    x_even = blk % 2 == 0
    for c in range(3):
        for q in range(5):
            for r in range(5):
                m = c * 25 + q * 5 + r
                ev, od = xe[m], xo[m]
                lo, hi = node(0, q, r), node(4, q, r)
                pr[c, lo, 0:2] = pr[c, lo, 0:2] + jnp.where(x_even, od, ev)
                pr[c, hi, 6:8] = pr[c, hi, 6:8] + jnp.where(x_even, ev, od)
    z_even = grp % 2 == 0
    zlo = [jnp.where(z_even, zo[g], ze[g]) for g in range(3)]
    zhi = [jnp.where(z_even, ze[g], zo[g]) for g in range(3)]

    xs[...] = jnp.zeros((128, 128), F32)
    slot4 = lax.broadcasted_iota(jnp.int32, (4, 128), 1) % 8
    for dg in (-1, 1):
        value = None
        for db in (-1, 1):
            ok = (grp + dg >= 0) & (grp + dg < N_GRP) & (blk + db >= 0) & (blk + db < N_BLK)
            at = jnp.where(ok, 8 * ((grp + dg) * N_BLK + blk + db), 0)
            part = ain[pl.ds(pl.multiple_of(at, 8), 4), :]
            part = jnp.where((slot4 >= 6) & ok, part, 0.0)
            value = roll(part, -6, 1) if value is None else value + part
        xs[pl.ds(31 if dg > 0 else 0, 4, stride=32), :] = value
    edges = xs[...].T
    for c in range(3):
        for p in range(5):
            for q in range(5):
                m = c * 25 + p * 5 + q
                n0, n4 = node(p, q, 0), node(p, q, 4)
                add0 = roll(zlo[m // 32], -(m % 32), 1)
                add4 = roll(zhi[m // 32], 31 - m % 32, 1)
                if p in (0, 4):
                    edge = edges[q * 24 + c * 8 : q * 24 + c * 8 + 8]
                    edge = jnp.where((sub < 4) == (p == 0), edge, 0.0)
                    add0, add4 = add0 + edge, add4 + edge
                pr[c, n0] = pr[c, n0] + jnp.where(k == 0, add0, 0.0)
                pr[c, n4] = pr[c, n4] + jnp.where(k == 31, add4, 0.0)

    odd_sub = sub % 2 == 1
    for c in range(3):
        for p in range(5):
            for r in range(5):
                sj[pl.ds(8 * (c * 32 + p * 5 + r), 8), :] = jnp.where(
                    odd_sub, pr[c, node(p, 0, r)], pr[c, node(p, 4, r)]
                )
    jump = fault_lanes(sj, 96)
    for i in range(4):
        ys[pl.ds(32 * i, 32), :] = ain[pl.ds(blk // 8 * 256 + 4 + i, 32, stride=8), :]
    par = ys[...].T
    t0x, t0z, scale_c, sigma_a = par[0:32], par[32:64], par[64:96], par[96:128]
    trial_x = t0x + ETA * jump[0:32]
    trial_z = t0z + ETA * jump[64:96]
    trial_norm, rate = solve(trial_x, trial_z, scale_c, sigma_a)
    keep = 1.0 - ETA * rate / jnp.maximum(trial_norm, TRACTION_FLOOR)
    push = (
        CORRECTION * (trial_x * keep - t0x),
        CORRECTION * ETA * jump[32:64],
        CORRECTION * (trial_z * keep - t0z),
    )
    for c in range(3):
        for i in range(4):
            sb[pl.ds(c * 256 + 2 * i + 1, 32, stride=8), :] = roll(push[c], -32 * i, 1)
            sb[pl.ds(c * 256 + 2 * i, 32, stride=8), :] = roll(push[c], 96 - 32 * i, 1)
    plus_at = (sub % 2 == 1) & (lane < 32)
    minus_at = (sub % 2 == 0) & (lane >= 96)
    for c in range(3):
        for p in range(5):
            for r in range(5):
                n0, n4 = node(p, 0, r), node(p, 4, r)
                push_back = sb[pl.ds(8 * (c * 32 + p * 5 + r), 8), :]
                pr[c, n0] = pr[c, n0] - jnp.where(plus_at, push_back, 0.0)
                pr[c, n4] = pr[c, n4] + jnp.where(minus_at, push_back, 0.0)
    for c in range(3):
        for n in range(125):
            v_out[c, n, :] = pr[c, n].reshape(1024)

    for u in range(4):
        for i in range(4):
            ys[pl.ds(8 * (u * 4 + i), 8), :] = ain[
                pl.ds(u * 256 + grp * 64 + i, 8, stride=8), :
            ]
    xs[...] = jnp.zeros((128, 128), F32)
    for u in range(4):
        for step, there, at, into in ((-1, grp > 0, 3, 0), (8, grp < N_GRP - 1, 0, 31)):
            source = jnp.where(there, (u * 32 + grp * 8 + step) * 8 + at, 0)
            value = ain[pl.ds(source, 1), :]
            xs[pl.ds(u * 32 + into, 1), :] = jnp.where(there, value, 0.0)
    body, ends = ys[...].T, xs[...].T
    first = jnp.where(grp_is(blk, 0), 1.0, 0.0).astype(F32)
    last = jnp.where(grp_is(blk, N_BLK - 1), 1.0, 0.0).astype(F32)

    def along_z(mat, p, c):
        at = p * 16 + c * 4
        t = mat[at : at + 8]
        low = jnp.where((sub == 0) & (lane >= 32), roll(roll(t, 32, 1), -5, 0), 0.0)
        high = jnp.where((sub == 4) & (lane < 96), roll(roll(t, -32, 1), -1, 0), 0.0)
        return t + low * first + high * last

    i_at, s_at = lane // 8 % 4, lane % 8
    for c in (0, 2):
        t = [along_z(body, p, c) for p in range(5)]
        end0, end4 = along_z(ends, 0, c), along_z(ends, 4, c)
        left = jnp.where(s_at == 0, end4, roll(t[4], -23, 1))
        right = jnp.where(s_at == 7, end0, roll(t[0], 23, 1))
        t[0], t[4] = (
            t[0] + jnp.where(i_at == 0, left, 0.0),
            t[4] + jnp.where(i_at == 3, right, 0.0),
        )
        for p in range(5):
            jp[c // 2, 5 * p : 5 * p + 5, :] = t[p][0:5]
    hot = slot_hot(slots[...])
    slot_jump = [
        lax.dot_general(
            jp[c], hot, (((1,), (0,)), ((), ())), precision=HIGHEST, preferred_element_type=F32
        )[0:25]
        for c in range(2)
    ]
    theta, a, b, length, pre_x, pre_z, sigma = (props[:, i, :] for i in range(7))
    scale_c = 0.5 * jnp.exp((FRICTION_REF + b * jnp.log(theta / length)) / a)
    _, rate = solve(
        pre_x + ETA * slot_jump[0], pre_z + ETA * slot_jump[1], scale_c, sigma * a
    )
    rate_out[...] = rate
    theta_out[...] = theta + DT * (1.0 - rate * theta / length)


def grp_is(index, value):
    return index == value


VMEM_LIMIT = 24 << 20


def shape(*dims):
    return jax.ShapeDtypeStruct(dims, F32)


def vmem(*dims):
    return pltpu.VMEM(dims, F32)


def force_call(*args):
    return pl.pallas_call(
        force_kernel,
        name="force",
        out_shape=(
            shape(3, 125, 8, 128), shape(75, 2, 128), shape(75, 2, 128),
            shape(3, 8, 128), shape(3, 8, 128), shape(1024, 128),
        ),
        scratch_shapes=[
            vmem(3, 125, 8, 128), vmem(3, 125, 8, 128), vmem(640, 128), vmem(128, 128),
            vmem(128, 128),
        ],
        compiler_params=pltpu.CompilerParams(vmem_limit_bytes=VMEM_LIMIT),
    )(*args)


def on_device(displacement, velocity, lame, fault_props, fault_slots):
    slots = fault_slots.reshape(1, 128)
    fault_props = jnp.transpose(fault_props, (1, 0, 2))
    f, xe, xo, ze, zo, abuf = force_call(displacement, velocity, lame, fault_props, slots)
    ain = lax.all_to_all(abuf, ("grp", "blk"), 0, 0, tiled=True)
    even_b = [(i, i ^ 1) for i in range(N_BLK)]
    odd_b = [(i, ((i + 1) ^ 1) - 1) for i in range(1, N_BLK - 1)]
    even_g = [(i, i ^ 1) for i in range(N_GRP)]
    odd_g = [(i, ((i + 1) ^ 1) - 1) for i in range(1, N_GRP - 1)]
    xe = lax.ppermute(xe, "blk", even_b)
    xo = lax.ppermute(xo, "blk", odd_b)
    ze = lax.ppermute(ze, "grp", even_g)
    zo = lax.ppermute(zo, "grp", odd_g)
    return pl.pallas_call(
        final_kernel,
        name="final",
        out_shape=(shape(3, 125, 1024), shape(25, 128), shape(25, 128)),
        scratch_shapes=[
            vmem(3, 125, 8, 128), vmem(768, 128), vmem(768, 128), vmem(128, 128),
            vmem(128, 128), vmem(2, 32, 128),
        ],
        compiler_params=pltpu.CompilerParams(vmem_limit_bytes=VMEM_LIMIT),
    )(f, velocity, xe, xo, ze, zo, ain, fault_props, slots)


def solution(mesh):
    both = ("grp", "blk")
    return jax.shard_map(
        on_device,
        mesh=mesh,
        in_specs=(P(None, None, both), P(None, None, both), P(None, both), P(None, None, both), P(both)),
        out_specs=(P(None, None, both), P(None, both), P(None, both)),
        check_vma=False,
    )
```

```python
import jax
import jax.numpy as jnp
import numpy as np
from jax import lax
from jax.experimental import pallas as pl
from jax.experimental.pallas import tpu as pltpu
from jax.sharding import PartitionSpec as P

NEWTON = 3
GLL_POINTS = np.array([-1.0, -np.sqrt(3.0 / 7.0), 0.0, np.sqrt(3.0 / 7.0), 1.0])
GLL_WEIGHTS = np.array([0.1, 49.0 / 90.0, 32.0 / 45.0, 49.0 / 90.0, 0.1])
DT = 0.01
W_END = 0.1
ETA = W_END / (2.0 * DT)
CORRECTION = DT / W_END
FRICTION_REF = 0.6
TRACTION_FLOOR = 1.0
N_GRP = 4
N_BLK = 32
F32 = jnp.float32
HIGHEST = lax.Precision.HIGHEST


def derivative_table():
    x = GLL_POINTS
    bary = [1.0 / np.prod([x[c] - x[o] for o in range(5) if o != c]) for c in range(5)]
    table = np.zeros((5, 5))
    for r in range(5):
        for c in range(5):
            if r != c:
                table[r, c] = bary[c] / bary[r] / (x[r] - x[c])
        table[r, r] = -np.sum(table[r])
    return table


D_TABLE = derivative_table()
M_TABLE = -DT * D_TABLE.T * GLL_WEIGHTS[None, :] / GLL_WEIGHTS[:, None]


def line(table, u):
    e0, e1 = u[0] + u[4], u[1] + u[3]
    o0, o1 = u[0] - u[4], u[1] - u[3]
    out = [None] * 5
    for i in range(2):
        even = (
            float((table[i, 0] + table[i, 4]) / 2) * e0
            + float((table[i, 1] + table[i, 3]) / 2) * e1
            + float(table[i, 2]) * u[2]
        )
        odd = (
            float((table[i, 0] - table[i, 4]) / 2) * o0
            + float((table[i, 1] - table[i, 3]) / 2) * o1
        )
        out[i] = odd + even
        out[4 - i] = odd - even
    out[2] = float(table[2, 0]) * o0 + float(table[2, 1]) * o1
    return out


def node(p, q, r):
    return 25 * p + 5 * q + r


def roll(x, shift, axis):
    shift = shift % x.shape[axis]
    return x if shift == 0 else pltpu.roll(x, shift, axis)


def row(ref, c, n):
    return ref[c, n, :].reshape(8, 128)


def tile_iota():
    lane = lax.broadcasted_iota(jnp.int32, (8, 128), 1)
    sub = lax.broadcasted_iota(jnp.int32, (8, 128), 0)
    return lane, sub, lane // 32, lane % 32, sub // 2


def inverse_sinh(value):
    return jnp.log(value + jnp.sqrt(1.0 + value * value))


def own_scales(grp, blk):
    half = lambda has: jnp.where(has, 0.5, 1.0).astype(F32)
    return half(blk > 0), half(blk < N_BLK - 1), half(grp > 0), half(grp < N_GRP - 1)


def slot_hot(slots):
    r = lax.broadcasted_iota(jnp.int32, (128, 128), 0)
    face = (r % 8) * 16 + (r // 8 % 4) * 4 + r // 32
    return (jnp.broadcast_to(slots, (128, 128)) == face).astype(F32)


def fault_lanes(ref, rows):
    block = lax.broadcasted_iota(jnp.int32, (rows, 128), 1) // 32
    plus = [roll(ref[pl.ds(2 * i + 1, rows, stride=8), :], 32 * i, 1) for i in range(4)]
    minus = [roll(ref[pl.ds(2 * i, rows, stride=8), :], 32 * i - 96, 1) for i in range(4)]
    out = plus[0] - minus[0]
    for i in range(1, 4):
        out = jnp.where(block == i, plus[i] - minus[i], out)
    return out


def force_kernel(
    disp_hbm, vel_hbm, lame_hbm, props_hbm, slots_hbm,
    f_out, xe_out, xo_out, abuf_hbm,
    gx, gy, sj, xs, disp, vel, lame, props, slots, abuf, sem_in, sem_out,
):
    grp = lax.axis_index("grp")
    blk = lax.axis_index("blk")
    pairs = [(disp_hbm.at[0], disp.at[0]), (lame_hbm, lame)]
    pairs += [(disp_hbm.at[1], disp.at[1]), (disp_hbm.at[2], disp.at[2])]
    pairs += [(props_hbm, props), (slots_hbm, slots)]
    pairs += [(vel_hbm.at[0], vel.at[0]), (vel_hbm.at[2], vel.at[1])]
    loads = [pltpu.make_async_copy(a, b, sem_in.at[t]) for t, (a, b) in enumerate(pairs)]
    for load in loads:
        load.start()
    lane, sub, jl, k, i_el = tile_iota()
    x0, x4, z0, z4 = own_scales(grp, blk)
    xs[...] = jnp.zeros((128, 128), F32)
    abuf[...] = jnp.zeros((640, 128), F32)
    loads[0].wait()

    for c in range(3):
        if c:
            loads[1 + c].wait()
        for r in range(5):
            u = [[row(disp, c, node(p, q, r)) for q in range(5)] for p in range(5)]
            for q in range(5):
                out = line(D_TABLE, [u[p][q] for p in range(5)])
                for p in range(5):
                    gx[c, node(p, q, r)] = out[p]
            for p in range(5):
                out = line(D_TABLE, u[p])
                for q in range(5):
                    gy[c, node(p, q, r)] = out[q]

    loads[4].wait()
    loads[5].wait()
    theta, a, b, length, pre_x, pre_z, sigma = (props[:, i, :] for i in range(7))
    xs[0:25] = pre_x
    xs[25:50] = pre_z
    xs[50:75] = 0.5 * jnp.exp((FRICTION_REF + b * jnp.log(theta / length)) / a)
    xs[75:100] = sigma * a
    packed = lax.dot_general(
        slot_hot(slots[...]), xs[...], (((1,), (1,)), ((), ())),
        precision=HIGHEST, preferred_element_type=F32,
    )
    for u in range(4):
        for i in range(4):
            t = u * 4 + i
            abuf[pl.ds(u * 160 + grp * 40 + i, 8, stride=5), :] = packed[8 * t : 8 * t + 8]

    loads[1].wait()
    lam = lame[0, :].reshape(8, 128)
    mu = lame[1, :].reshape(8, 128)
    mu2 = mu + mu
    for p in range(5):
        for q in range(5):
            gz = [
                line(D_TABLE, [row(disp, c, node(p, q, r)) for r in range(5)]) for c in range(3)
            ]
            sz = [[None] * 5 for _ in range(3)]
            for r in range(5):
                n = node(p, q, r)
                g0 = [gx[c, n] for c in range(3)]
                g1 = [gy[c, n] for c in range(3)]
                g2 = [gz[c][r] for c in range(3)]
                spread = lam * (g0[0] + g1[1] + g2[2])
                s01 = mu * (g0[1] + g1[0])
                s02 = mu * (g0[2] + g2[0])
                s12 = mu * (g1[2] + g2[1])
                gx[0, n] = spread + mu2 * g0[0]
                gx[1, n] = s01
                gx[2, n] = s02
                gy[1, n] = spread + mu2 * g1[1]
                gy[2, n] = s12
                sz[0][r], sz[1][r], sz[2][r] = s02, s12, spread + mu2 * g2[2]
            for c in range(3):
                out = line(M_TABLE, sz[c])
                for r in range(5):
                    f_out[c, node(p, q, r)] = out[r]

    y4_in, y0_in = jl < 3, jl > 0
    x4_in, x0_in = i_el < 3, i_el > 0
    z4_in, z0_in = k < 31, k > 0
    zero = jnp.zeros((8, 128), F32)

    def xy_parts(c, r):
        f = [[f_out[c, node(p, q, r)] for q in range(5)] for p in range(5)]
        for p in range(5):
            if c == 0:
                s = [gx[1, node(p, q, r)] for q in range(5)]
            else:
                s = [gy[c, node(p, q, r)] for q in range(5)]
            out = line(M_TABLE, s)
            for q in range(5):
                f[p][q] = f[p][q] + out[q]
        for q in range(5):
            out = line(M_TABLE, [gx[c, node(p, q, r)] for p in range(5)])
            for p in range(5):
                f[p][q] = f[p][q] + out[p]
        for p in range(5):
            up, down = roll(f[p][0], -32, 1), roll(f[p][4], 32, 1)
            f[p][0], f[p][4] = (
                jnp.where(y0_in, 0.5 * (f[p][0] + down), f[p][0]),
                jnp.where(y4_in, 0.5 * (f[p][4] + up), f[p][4]),
            )
        for q in range(5):
            avg = 0.5 * (f[4][q] + roll(f[0][q], -2, 0))
            f[0][q] = jnp.where(x0_in, roll(avg, 2, 0), f[0][q] * x0)
            f[4][q] = jnp.where(x4_in, avg, f[4][q] * x4)
        for p in range(5):
            for q in range(5):
                f_out[c, node(p, q, r)] = f[p][q]

    for c in range(3):
        xy_parts(c, 0)
        xy_parts(c, 4)
        for p in range(5):
            for q in range(5):
                n0, n4 = node(p, q, 0), node(p, q, 4)
                a0, a4 = f_out[c, n0], f_out[c, n4]
                up, down = roll(a0, -1, 1), roll(a4, 1, 1)
                f_out[c, n0] = jnp.where(z0_in, 0.5 * (a0 + down), a0 * z0)
                f_out[c, n4] = jnp.where(z4_in, 0.5 * (a4 + up), a4 * z4)
        for r in (1, 2, 3):
            xy_parts(c, r)

    loads[6].wait()
    loads[7].wait()
    own_x = {0: jnp.where(x0_in, 1.0, x0), 4: jnp.where(x4_in, 1.0, x4)}
    own_z = {0: jnp.where(z0_in, 1.0, z0), 4: jnp.where(z4_in, 1.0, z4)}
    odd_sub = sub % 2 == 1
    for p in range(5):
        for cc in range(2):
            c = 2 * cc
            at = 6 * (2 * p + cc)
            sides = [None] * 5
            for r in range(5):
                own = None
                for part in (own_x.get(p), own_z.get(r)):
                    if part is not None:
                        own = part if own is None else own * part
                n0, n4 = node(p, 0, r), node(p, 4, r)
                v = jnp.where(odd_sub, row(vel, cc, n0), row(vel, cc, n4))
                f = jnp.where(odd_sub, f_out[c, n0], f_out[c, n4])
                sides[r] = f + (v if own is None else v * own)
                sj[pl.ds(8 * (at + r), 8), :] = sides[r]
            extra = jnp.where(k == 0, roll(sides[4], -31, 1), 0.0)
            extra = jnp.where(k == 31, roll(sides[0], 31, 1), extra)
            sj[pl.ds(8 * (at + 5), 8), :] = extra
    for t in range(60, 64):
        sj[pl.ds(8 * t, 8), :] = zero
    y = fault_lanes(sj, 64)
    yt = jnp.concatenate([y, jnp.zeros((64, 128), F32)]).T
    dest = blk // 8
    lane32 = lax.broadcasted_iota(jnp.int32, (32, 128), 1)
    tails = [roll(yt[32 * i : 32 * i + 32], 68, 1) for i in range(4)]
    heads = yt[0:32]
    for i in range(1, 4):
        heads = jnp.where(lane32 // 32 == i, roll(yt[32 * i : 32 * i + 32], 32 * i, 1), heads)

    def put_jump(d):
        for i in range(4):
            rows = pl.ds(d * 160 + i, 32, stride=5)
            abuf[rows, :] = jnp.where(lane32 >= 100, tails[i], abuf[rows, :])
        abuf[pl.ds(d * 160 + 4, 32, stride=5), :] = heads

    put_jump(dest)

    @pl.when((blk % 8 == 7) & (dest < N_GRP - 1))
    def _():
        put_jump(dest + 1)

    @pl.when((blk % 8 == 0) & (dest > 0))
    def _():
        put_jump(dest - 1)

    stores = []
    for t in range(4):
        rows = pl.ds(160 * t, 160)
        stores.append(pltpu.make_async_copy(abuf.at[rows], abuf_hbm.at[rows], sem_out.at[t]))
    for copy in stores:
        copy.start()

    x_even = blk % 2 == 0
    for c in range(3):
        for q in range(5):
            for r in range(5):
                m = c * 25 + q * 5 + r
                lo = f_out[c, node(0, q, r)]
                hi = roll(f_out[c, node(4, q, r)], 2, 0)
                xe_out[m] = jnp.where(x_even, hi, lo)[0:2]
                xo_out[m] = jnp.where(x_even, lo, hi)[0:2]
    for copy in stores:
        copy.wait()


def middle_kernel(f_in, vel_hbm, xe, xo, p_out, ze_out, zo_out, vel, sem):
    grp = lax.axis_index("grp")
    blk = lax.axis_index("blk")
    lane, sub, jl, k, i_el = tile_iota()
    loads = [pltpu.make_async_copy(vel_hbm.at[c], vel.at[c], sem.at[c]) for c in range(3)]
    for load in loads:
        load.start()
    x_even = blk % 2 == 0
    for c in range(3):
        for n in range(125):
            p_out[c, n] = f_in[c, n]
        for q in range(5):
            for r in range(5):
                m = c * 25 + q * 5 + r
                ev, od = xe[m], xo[m]
                lo, hi = node(0, q, r), node(4, q, r)
                p_out[c, lo, 0:2] = p_out[c, lo, 0:2] + jnp.where(x_even, od, ev)
                p_out[c, hi, 6:8] = p_out[c, hi, 6:8] + jnp.where(x_even, ev, od)
    z_even = grp % 2 == 0
    for g in range(3):
        zlo = zhi = jnp.zeros((8, 128), F32)
        for m in range(32 * g, min(75, 32 * g + 32)):
            c, pq = m // 25, m % 25
            at = k == m % 32
            zlo = jnp.where(at, roll(p_out[c, 5 * pq], m % 32, 1), zlo)
            zhi = jnp.where(at, roll(p_out[c, 5 * pq + 4], m % 32 - 31, 1), zhi)
        ze_out[g] = jnp.where(z_even, zhi, zlo)
        zo_out[g] = jnp.where(z_even, zlo, zhi)
    for c in range(3):
        loads[c].wait()
        for n in range(125):
            p_out[c, n] = p_out[c, n] + row(vel, c, n)


def halo_kernel(p_in, ze, zo, p_out, jump_out, sj):
    grp = lax.axis_index("grp")
    lane, sub, jl, k, i_el = tile_iota()
    z_even = grp % 2 == 0
    zlo = [jnp.where(z_even, zo[g], ze[g]) for g in range(3)]
    zhi = [jnp.where(z_even, ze[g], zo[g]) for g in range(3)]
    for c in range(3):
        for p in range(5):
            for q in range(5):
                m = c * 25 + p * 5 + q
                n0, n4 = node(p, q, 0), node(p, q, 4)
                add0 = roll(zlo[m // 32], -(m % 32), 1)
                add4 = roll(zhi[m // 32], 31 - m % 32, 1)
                p_out[c, n0] = p_in[c, n0] + jnp.where(k == 0, add0, 0.0)
                p_out[c, n4] = p_in[c, n4] + jnp.where(k == 31, add4, 0.0)
                for r in (1, 2, 3):
                    p_out[c, node(p, q, r)] = p_in[c, node(p, q, r)]
    odd_sub = sub % 2 == 1
    for c in range(3):
        for p in range(5):
            for r in range(5):
                sj[pl.ds(8 * (c * 32 + p * 5 + r), 8), :] = jnp.where(
                    odd_sub, p_out[c, node(p, 0, r)], p_out[c, node(p, 4, r)]
                )
        for t in range(25, 32):
            sj[pl.ds(8 * (c * 32 + t), 8), :] = jnp.zeros((8, 128), F32)
    jump_out[...] = fault_lanes(sj, 96)


def solve(trial_x, trial_z, scale_c, sigma_a):
    trial_norm = jnp.sqrt(trial_x * trial_x + trial_z * trial_z)
    rate = jnp.zeros_like(trial_norm)
    for _ in range(NEWTON):
        arg = scale_c * rate
        residual = trial_norm - ETA * rate - sigma_a * inverse_sinh(arg)
        slope = -ETA - sigma_a * scale_c / jnp.sqrt(1.0 + arg * arg)
        rate = rate - residual / slope
    return trial_norm, rate


def final_kernel(
    p_in, jump, ain, props, slots,
    v_hbm, rate_out, theta_out,
    sb, xs, ys, jp, v_out, sem,
):
    grp = lax.axis_index("grp")
    blk = lax.axis_index("blk")
    lane, sub, jl, k, i_el = tile_iota()

    for i in range(4):
        ys[pl.ds(32 * i, 32), :] = ain[pl.ds(blk // 8 * 160 + i, 32, stride=5), :]
    ys[...] = ys[...].T
    t0x, t0z, scale_c, sigma_a = (ys[pl.ds(25 * j, 32), :] for j in range(4))
    trial_x = t0x + ETA * jump[0:32]
    trial_z = t0z + ETA * jump[64:96]
    trial_norm, rate = solve(trial_x, trial_z, scale_c, sigma_a)
    keep = 1.0 - ETA * rate / jnp.maximum(trial_norm, TRACTION_FLOOR)
    push = (
        CORRECTION * (trial_x * keep - t0x),
        CORRECTION * ETA * jump[32:64],
        CORRECTION * (trial_z * keep - t0z),
    )
    for c in range(3):
        for i in range(4):
            sb[pl.ds(c * 256 + 2 * i + 1, 32, stride=8), :] = roll(push[c], -32 * i, 1)
            sb[pl.ds(c * 256 + 2 * i, 32, stride=8), :] = roll(push[c], 96 - 32 * i, 1)
    plus_at = (sub % 2 == 1) & (lane < 32)
    minus_at = (sub % 2 == 0) & (lane >= 96)
    stores = []
    for c in range(3):
        for p in range(5):
            for r in range(5):
                n0, n4 = node(p, 0, r), node(p, 4, r)
                push_back = sb[pl.ds(8 * (c * 32 + p * 5 + r), 8), :]
                v_out[c, n0, :] = (p_in[c, n0] - jnp.where(plus_at, push_back, 0.0)).reshape(1024)
                v_out[c, n4, :] = (p_in[c, n4] + jnp.where(minus_at, push_back, 0.0)).reshape(1024)
                for q in (1, 2, 3):
                    v_out[c, node(p, q, r), :] = p_in[c, node(p, q, r)].reshape(1024)
        stores.append(pltpu.make_async_copy(v_out.at[c], v_hbm.at[c], sem.at[c]))
        stores[c].start()

    for u in range(4):
        heads = ain[pl.ds(u * 160 + grp * 40 + 4, 8, stride=5), :]
        for i in range(4):
            tails = roll(ain[pl.ds(u * 160 + grp * 40 + i, 8, stride=5), :], 60, 1)
            both = jnp.where(lane < 32, roll(heads, -32 * i, 1), tails)
            ys[pl.ds(8 * (u * 4 + i), 8), :] = jnp.where(lane < 60, both, 0.0)
    xs[...] = jnp.zeros((128, 128), F32)
    lane4 = lax.broadcasted_iota(jnp.int32, (4, 128), 1)
    for step, there, i, into in ((-1, grp > 0, 3, 0), (8, grp < N_GRP - 1, 0, 31)):
        first_row = jnp.where(there, (grp * 8 + step) * 5, 0)
        tails = roll(ain[pl.ds(first_row + i, 4, stride=160), :], 60, 1)
        heads = roll(ain[pl.ds(first_row + 4, 4, stride=160), :], -32 * i, 1)
        both = jnp.where(lane4 < 32, heads, tails)
        xs[pl.ds(into, 4, stride=32), :] = jnp.where((lane4 < 60) & there, both, 0.0)
    ys[...] = ys[...].T
    xs[...] = xs[...].T
    first = jnp.where(grp_is(blk, 0), 1.0, 0.0).astype(F32)
    last = jnp.where(grp_is(blk, N_BLK - 1), 1.0, 0.0).astype(F32)

    def along_z(mat, p, c):
        t = mat[pl.ds(6 * (2 * p + c // 2), 8), :]
        low = jnp.where((sub == 0) & (lane >= 32), roll(roll(t, 32, 1), -5, 0), 0.0)
        high = jnp.where((sub == 4) & (lane < 96), roll(roll(t, -32, 1), -1, 0), 0.0)
        return t + low * first + high * last

    i_at, s_at = lane // 8 % 4, lane % 8
    for c in (0, 2):
        t = [along_z(ys, p, c) for p in range(5)]
        end0, end4 = along_z(xs, 0, c), along_z(xs, 4, c)
        left = jnp.where(s_at == 0, end4, roll(t[4], -23, 1))
        right = jnp.where(s_at == 7, end0, roll(t[0], 23, 1))
        t[0], t[4] = (
            t[0] + jnp.where(i_at == 0, left, 0.0),
            t[4] + jnp.where(i_at == 3, right, 0.0),
        )
        for p in range(5):
            jp[c // 2, 5 * p : 5 * p + 5, :] = t[p][0:5]
    hot = slot_hot(slots[...])
    slot_jump = [
        lax.dot_general(
            jp[c], hot, (((1,), (0,)), ((), ())), precision=HIGHEST, preferred_element_type=F32
        )[0:25]
        for c in range(2)
    ]
    theta, a, b, length, pre_x, pre_z, sigma = (props[:, i, :] for i in range(7))
    scale_c = 0.5 * jnp.exp((FRICTION_REF + b * jnp.log(theta / length)) / a)
    _, rate = solve(
        pre_x + ETA * slot_jump[0], pre_z + ETA * slot_jump[1], scale_c, sigma * a
    )
    rate_out[...] = rate
    theta_out[...] = theta + DT * (1.0 - rate * theta / length)
    for copy in stores:
        copy.wait()


def grp_is(index, value):
    return index == value


VMEM_LIMIT = 24 << 20


def shape(*dims):
    return jax.ShapeDtypeStruct(dims, F32)


def vmem(*dims):
    return pltpu.VMEM(dims, F32)


HBM = pl.BlockSpec(memory_space=pltpu.HBM)
WHOLE = pl.BlockSpec(memory_space=pltpu.VMEM)


PARAMS = pltpu.CompilerParams(vmem_limit_bytes=VMEM_LIMIT)
FIELD = (3, 125, 8, 128)


def in_hbm(x):
    return pltpu.with_memory_space_constraint(x, pltpu.HBM)


def force_call(*args):
    return pl.pallas_call(
        force_kernel,
        name="force",
        in_specs=[HBM] * 5,
        out_specs=[WHOLE] * 3 + [HBM],
        out_shape=(
            shape(*FIELD), shape(75, 2, 128), shape(75, 2, 128), pltpu.HBM((640, 128), F32),
        ),
        scratch_shapes=[
            vmem(*FIELD), vmem(*FIELD), vmem(512, 128), vmem(128, 128),
            vmem(3, 125, 1024), vmem(2, 125, 1024), vmem(2, 1024),
            vmem(25, 7, 128), pltpu.VMEM((1, 128), jnp.int32), vmem(640, 128),
            pltpu.SemaphoreType.DMA((8,)), pltpu.SemaphoreType.DMA((4,)),
        ],
        compiler_params=PARAMS,
    )(*[in_hbm(x) for x in args])


def on_device(displacement, velocity, lame, fault_props, fault_slots):
    slots = fault_slots.reshape(1, 128)
    fault_props = jnp.transpose(fault_props, (1, 0, 2))
    even_b = [(i, i ^ 1) for i in range(N_BLK)]
    odd_b = [(i, ((i + 1) ^ 1) - 1) for i in range(1, N_BLK - 1)]
    even_g = [(i, i ^ 1) for i in range(N_GRP)]
    odd_g = [(i, ((i + 1) ^ 1) - 1) for i in range(1, N_GRP - 1)]
    f, xe, xo, abuf = force_call(displacement, velocity, lame, fault_props, slots)
    ain = lax.all_to_all(abuf.reshape(640, 1, 128), ("grp", "blk"), 0, 0, tiled=True)
    ain = ain.reshape(640, 128)
    xe = lax.ppermute(xe, "blk", even_b)
    xo = lax.ppermute(xo, "blk", odd_b)
    p, ze, zo = pl.pallas_call(
        middle_kernel,
        name="middle",
        in_specs=[WHOLE, HBM, WHOLE, WHOLE],
        out_specs=[WHOLE] * 3,
        out_shape=(shape(*FIELD), shape(3, 8, 128), shape(3, 8, 128)),
        scratch_shapes=[vmem(3, 125, 1024), pltpu.SemaphoreType.DMA((3,))],
        compiler_params=PARAMS,
    )(f, in_hbm(velocity), xe, xo)
    ze = lax.ppermute(ze, "grp", even_g)
    zo = lax.ppermute(zo, "grp", odd_g)
    p, jump = pl.pallas_call(
        halo_kernel,
        name="halo",
        in_specs=[WHOLE] * 3,
        out_specs=[WHOLE] * 2,
        out_shape=(shape(*FIELD), shape(96, 128)),
        scratch_shapes=[vmem(768, 128)],
        compiler_params=PARAMS,
    )(p, ze, zo)
    return pl.pallas_call(
        final_kernel,
        name="final",
        in_specs=[WHOLE] * 5,
        out_specs=[HBM, WHOLE, WHOLE],
        out_shape=(pltpu.HBM((3, 125, 1024), F32), shape(25, 128), shape(25, 128)),
        scratch_shapes=[
            vmem(768, 128), vmem(128, 128), vmem(128, 128), vmem(2, 32, 128),
            vmem(3, 125, 1024), pltpu.SemaphoreType.DMA((3,)),
        ],
        compiler_params=PARAMS,
    )(p, jump, ain, fault_props, slots)


def solution(mesh):
    both = ("grp", "blk")
    return jax.shard_map(
        on_device,
        mesh=mesh,
        in_specs=(P(None, None, both), P(None, None, both), P(None, both), P(None, None, both), P(both)),
        out_specs=(P(None, None, both), P(None, both), P(None, both)),
        check_vma=False,
    )
```

```python
import jax
import jax.numpy as jnp
import numpy as np
from jax import lax
from jax.experimental import pallas as pl
from jax.experimental.pallas import tpu as pltpu
from jax.sharding import PartitionSpec as P

NEWTON = 3
GLL_POINTS = np.array([-1.0, -np.sqrt(3.0 / 7.0), 0.0, np.sqrt(3.0 / 7.0), 1.0])
GLL_WEIGHTS = np.array([0.1, 49.0 / 90.0, 32.0 / 45.0, 49.0 / 90.0, 0.1])
DT = 0.01
W_END = 0.1
ETA = W_END / (2.0 * DT)
CORRECTION = DT / W_END
FRICTION_REF = 0.6
TRACTION_FLOOR = 1.0
N_GRP = 4
N_BLK = 32
F32 = jnp.float32
HIGHEST = lax.Precision.HIGHEST


def derivative_table():
    x = GLL_POINTS
    bary = [1.0 / np.prod([x[c] - x[o] for o in range(5) if o != c]) for c in range(5)]
    table = np.zeros((5, 5))
    for r in range(5):
        for c in range(5):
            if r != c:
                table[r, c] = bary[c] / bary[r] / (x[r] - x[c])
        table[r, r] = -np.sum(table[r])
    return table


D_TABLE = derivative_table()
M_TABLE = -DT * D_TABLE.T * GLL_WEIGHTS[None, :] / GLL_WEIGHTS[:, None]


def line(table, u):
    e0, e1 = u[0] + u[4], u[1] + u[3]
    o0, o1 = u[0] - u[4], u[1] - u[3]
    out = [None] * 5
    for i in range(2):
        even = (
            float((table[i, 0] + table[i, 4]) / 2) * e0
            + float((table[i, 1] + table[i, 3]) / 2) * e1
            + float(table[i, 2]) * u[2]
        )
        odd = (
            float((table[i, 0] - table[i, 4]) / 2) * o0
            + float((table[i, 1] - table[i, 3]) / 2) * o1
        )
        out[i] = odd + even
        out[4 - i] = odd - even
    out[2] = float(table[2, 0]) * o0 + float(table[2, 1]) * o1
    return out


def node(p, q, r):
    return 25 * p + 5 * q + r


def roll(x, shift, axis):
    shift = shift % x.shape[axis]
    return x if shift == 0 else pltpu.roll(x, shift, axis)


def row(ref, c, n):
    return ref[c, n, :].reshape(8, 128)


def tile_iota():
    lane = lax.broadcasted_iota(jnp.int32, (8, 128), 1)
    sub = lax.broadcasted_iota(jnp.int32, (8, 128), 0)
    return lane, sub, lane // 32, lane % 32, sub // 2


def inverse_sinh(value):
    return jnp.log(value + jnp.sqrt(1.0 + value * value))


def own_scales(grp, blk):
    half = lambda has: jnp.where(has, 0.5, 1.0).astype(F32)
    return half(blk > 0), half(blk < N_BLK - 1), half(grp > 0), half(grp < N_GRP - 1)


def slot_hot(slots):
    r = lax.broadcasted_iota(jnp.int32, (128, 128), 0)
    face = (r % 8) * 16 + (r // 8 % 4) * 4 + r // 32
    return (jnp.broadcast_to(slots, (128, 128)) == face).astype(F32)


def fault_lanes(ref, rows):
    block = lax.broadcasted_iota(jnp.int32, (rows, 128), 1) // 32
    plus = [roll(ref[pl.ds(2 * i + 1, rows, stride=8), :], 32 * i, 1) for i in range(4)]
    minus = [roll(ref[pl.ds(2 * i, rows, stride=8), :], 32 * i - 96, 1) for i in range(4)]
    out = plus[0] - minus[0]
    for i in range(1, 4):
        out = jnp.where(block == i, plus[i] - minus[i], out)
    return out


def force_kernel(
    disp_hbm, vel_hbm, lame_hbm, props_hbm, slots_hbm,
    f_out, xe_out, xo_out, ze_out, zo_out, abuf_hbm,
    gx, gy, sj, xs, disp, vel, lame, props, slots, abuf, sem_in, sem_out,
):
    grp = lax.axis_index("grp")
    blk = lax.axis_index("blk")
    pairs = [(disp_hbm.at[0], disp.at[0]), (lame_hbm, lame)]
    pairs += [(disp_hbm.at[1], disp.at[1]), (disp_hbm.at[2], disp.at[2])]
    pairs += [(props_hbm, props), (slots_hbm, slots)]
    pairs += [(vel_hbm.at[0], vel.at[0]), (vel_hbm.at[2], vel.at[1])]
    loads = [pltpu.make_async_copy(a, b, sem_in.at[t]) for t, (a, b) in enumerate(pairs)]
    for load in loads:
        load.start()
    lane, sub, jl, k, i_el = tile_iota()
    x0, x4, z0, z4 = own_scales(grp, blk)
    xs[...] = jnp.zeros((128, 128), F32)
    abuf[...] = jnp.zeros((768, 128), F32)
    loads[0].wait()

    for c in range(3):
        if c:
            loads[1 + c].wait()
        for r in range(5):
            u = [[row(disp, c, node(p, q, r)) for q in range(5)] for p in range(5)]
            for q in range(5):
                out = line(D_TABLE, [u[p][q] for p in range(5)])
                for p in range(5):
                    gx[c, node(p, q, r)] = out[p]
            for p in range(5):
                out = line(D_TABLE, u[p])
                for q in range(5):
                    gy[c, node(p, q, r)] = out[q]

    loads[4].wait()
    loads[5].wait()
    theta, a, b, length, pre_x, pre_z, sigma = (props[:, i, :] for i in range(7))
    xs[0:25] = pre_x
    xs[25:50] = pre_z
    xs[50:75] = 0.5 * jnp.exp((FRICTION_REF + b * jnp.log(theta / length)) / a)
    xs[75:100] = sigma * a
    packed = lax.dot_general(
        slot_hot(slots[...]), xs[...], (((1,), (1,)), ((), ())),
        precision=HIGHEST, preferred_element_type=F32,
    )
    for u in range(4):
        for i in range(4):
            t = u * 4 + i
            abuf[pl.ds(u * 192 + grp * 48 + i, 8, stride=6), :] = packed[8 * t : 8 * t + 8]

    loads[1].wait()
    lam = lame[0, :].reshape(8, 128)
    mu = lame[1, :].reshape(8, 128)
    mu2 = mu + mu
    for p in range(5):
        for q in range(5):
            gz = [
                line(D_TABLE, [row(disp, c, node(p, q, r)) for r in range(5)]) for c in range(3)
            ]
            sz = [[None] * 5 for _ in range(3)]
            for r in range(5):
                n = node(p, q, r)
                g0 = [gx[c, n] for c in range(3)]
                g1 = [gy[c, n] for c in range(3)]
                g2 = [gz[c][r] for c in range(3)]
                spread = lam * (g0[0] + g1[1] + g2[2])
                s01 = mu * (g0[1] + g1[0])
                s02 = mu * (g0[2] + g2[0])
                s12 = mu * (g1[2] + g2[1])
                gx[0, n] = spread + mu2 * g0[0]
                gx[1, n] = s01
                gx[2, n] = s02
                gy[1, n] = spread + mu2 * g1[1]
                gy[2, n] = s12
                sz[0][r], sz[1][r], sz[2][r] = s02, s12, spread + mu2 * g2[2]
            for c in range(3):
                out = line(M_TABLE, sz[c])
                for r in range(5):
                    f_out[c, node(p, q, r)] = out[r]

    y4_in, y0_in = jl < 3, jl > 0
    x4_in, x0_in = i_el < 3, i_el > 0
    z4_in, z0_in = k < 31, k > 0
    zero = jnp.zeros((8, 128), F32)

    def xy_parts(c, r):
        f = [[f_out[c, node(p, q, r)] for q in range(5)] for p in range(5)]
        for p in range(5):
            if c == 0:
                s = [gx[1, node(p, q, r)] for q in range(5)]
            else:
                s = [gy[c, node(p, q, r)] for q in range(5)]
            out = line(M_TABLE, s)
            for q in range(5):
                f[p][q] = f[p][q] + out[q]
        for q in range(5):
            out = line(M_TABLE, [gx[c, node(p, q, r)] for p in range(5)])
            for p in range(5):
                f[p][q] = f[p][q] + out[p]
        for p in range(5):
            up, down = roll(f[p][0], -32, 1), roll(f[p][4], 32, 1)
            f[p][0], f[p][4] = (
                jnp.where(y0_in, 0.5 * (f[p][0] + down), f[p][0]),
                jnp.where(y4_in, 0.5 * (f[p][4] + up), f[p][4]),
            )
        for q in range(5):
            avg = 0.5 * (f[4][q] + roll(f[0][q], -2, 0))
            f[0][q] = jnp.where(x0_in, roll(avg, 2, 0), f[0][q] * x0)
            f[4][q] = jnp.where(x4_in, avg, f[4][q] * x4)
        for p in range(5):
            for q in range(5):
                f_out[c, node(p, q, r)] = f[p][q]

    for c in range(3):
        xy_parts(c, 0)
        xy_parts(c, 4)
        for p in range(5):
            for q in range(5):
                n0, n4 = node(p, q, 0), node(p, q, 4)
                a0, a4 = f_out[c, n0], f_out[c, n4]
                up, down = roll(a0, -1, 1), roll(a4, 1, 1)
                f_out[c, n0] = jnp.where(z0_in, 0.5 * (a0 + down), a0 * z0)
                f_out[c, n4] = jnp.where(z4_in, 0.5 * (a4 + up), a4 * z4)
        for r in (1, 2, 3):
            xy_parts(c, r)

    loads[6].wait()
    loads[7].wait()
    own_x = {0: jnp.where(x0_in, 1.0, x0), 4: jnp.where(x4_in, 1.0, x4)}
    own_z = {0: jnp.where(z0_in, 1.0, z0), 4: jnp.where(z4_in, 1.0, z4)}
    odd_sub = sub % 2 == 1
    for p in range(5):
        for cc in range(2):
            c = 2 * cc
            at = 6 * (2 * p + cc)
            sides = [None] * 5
            for r in range(5):
                own = None
                for part in (own_x.get(p), own_z.get(r)):
                    if part is not None:
                        own = part if own is None else own * part
                n0, n4 = node(p, 0, r), node(p, 4, r)
                v = jnp.where(odd_sub, row(vel, cc, n0), row(vel, cc, n4))
                f = jnp.where(odd_sub, f_out[c, n0], f_out[c, n4])
                sides[r] = f + (v if own is None else v * own)
                sj[pl.ds(8 * (at + r), 8), :] = sides[r]
            extra = jnp.where(k == 0, roll(sides[4], -31, 1), 0.0)
            extra = jnp.where(k == 31, roll(sides[0], 31, 1), extra)
            sj[pl.ds(8 * (at + 5), 8), :] = extra
    for t in range(60, 64):
        sj[pl.ds(8 * t, 8), :] = zero
    y = fault_lanes(sj, 64)
    yt = jnp.concatenate([y, jnp.zeros((64, 128), F32)]).T
    dest = blk // 8
    lane32 = lax.broadcasted_iota(jnp.int32, (32, 128), 1)
    tails = [roll(yt[32 * i : 32 * i + 32], 68, 1) for i in range(4)]
    heads = yt[0:32]
    for i in range(1, 4):
        heads = jnp.where(lane32 // 32 == i, roll(yt[32 * i : 32 * i + 32], 32 * i, 1), heads)

    def put_jump(d):
        for i in range(4):
            rows = pl.ds(d * 192 + i, 32, stride=6)
            abuf[rows, :] = jnp.where(lane32 >= 100, tails[i], abuf[rows, :])
        abuf[pl.ds(d * 192 + 4, 32, stride=6), :] = heads

    put_jump(dest)

    @pl.when((blk % 8 == 7) & (dest < N_GRP - 1))
    def _():
        put_jump(dest + 1)

    @pl.when((blk % 8 == 0) & (dest > 0))
    def _():
        put_jump(dest - 1)

    for dg in (-1, 1):
        edge = zero
        for m in range(15):
            c, q = m // 5, m % 5
            r = 4 if dg > 0 else 0
            value = jnp.where(sub < 4, f_out[c, node(0, q, r)], f_out[c, node(4, q, r)])
            edge = jnp.where(k == m, roll(value, m - (31 if dg > 0 else 0), 1), edge)
        edge = jnp.where(k < 15, edge, roll(roll(edge, 15, 1), -1, 0))
        for db, at in ((-1, 0), (1, 6)):
            to_g, to_b = grp + dg, blk + db
            there = (to_g >= 0) & (to_g < N_GRP) & (to_b >= 0) & (to_b < N_BLK)

            @pl.when(there)
            def _(edge=edge, at=at, to_g=to_g, to_b=to_b):
                abuf[pl.ds(6 * (to_g * N_BLK + to_b) + 5, 1), :] = edge[at : at + 1]

    stores = []
    for t in range(4):
        rows = pl.ds(192 * t, 192)
        stores.append(pltpu.make_async_copy(abuf.at[rows], abuf_hbm.at[rows], sem_out.at[t]))
    for copy in stores:
        copy.start()

    x_even = blk % 2 == 0
    for c in range(3):
        for q in range(5):
            for r in range(5):
                m = c * 25 + q * 5 + r
                lo = f_out[c, node(0, q, r)]
                hi = roll(f_out[c, node(4, q, r)], 2, 0)
                xe_out[m] = jnp.where(x_even, hi, lo)[0:2]
                xo_out[m] = jnp.where(x_even, lo, hi)[0:2]

    z_even = grp % 2 == 0
    for g in range(3):
        zlo = zhi = jnp.zeros((8, 128), F32)
        for m in range(32 * g, min(75, 32 * g + 32)):
            c, pq = m // 25, m % 25
            at = k == m % 32
            zlo = jnp.where(at, roll(f_out[c, 5 * pq], m % 32, 1), zlo)
            zhi = jnp.where(at, roll(f_out[c, 5 * pq + 4], m % 32 - 31, 1), zhi)
        ze_out[g] = jnp.where(z_even, zhi, zlo)
        zo_out[g] = jnp.where(z_even, zlo, zhi)
    for copy in stores:
        copy.wait()


def halo_kernel(f_in, vel_hbm, xe, xo, ze, zo, p_out, vel, sem):
    grp = lax.axis_index("grp")
    blk = lax.axis_index("blk")
    lane, sub, jl, k, i_el = tile_iota()
    loads = [pltpu.make_async_copy(vel_hbm.at[c], vel.at[c], sem.at[c]) for c in range(3)]
    for load in loads:
        load.start()
    x_even = blk % 2 == 0
    z_even = grp % 2 == 0
    zlo = [jnp.where(z_even, zo[g], ze[g]) for g in range(3)]
    zhi = [jnp.where(z_even, ze[g], zo[g]) for g in range(3)]
    for c in range(3):
        loads[c].wait()
        for p in range(5):
            for q in range(5):
                m = c * 25 + p * 5 + q
                add0 = roll(zlo[m // 32], -(m % 32), 1)
                add4 = roll(zhi[m // 32], 31 - m % 32, 1)
                for r in range(5):
                    n = node(p, q, r)
                    value = f_in[c, n] + row(vel, c, n)
                    if r == 0:
                        value = value + jnp.where(k == 0, add0, 0.0)
                    if r == 4:
                        value = value + jnp.where(k == 31, add4, 0.0)
                    p_out[c, n] = value
        for q in range(5):
            for r in range(5):
                m = c * 25 + q * 5 + r
                ev, od = xe[m], xo[m]
                lo, hi = node(0, q, r), node(4, q, r)
                p_out[c, lo, 0:2] = p_out[c, lo, 0:2] + jnp.where(x_even, od, ev)
                p_out[c, hi, 6:8] = p_out[c, hi, 6:8] + jnp.where(x_even, ev, od)


def solve(trial_x, trial_z, scale_c, sigma_a):
    trial_norm = jnp.sqrt(trial_x * trial_x + trial_z * trial_z)
    rate = jnp.zeros_like(trial_norm)
    for _ in range(NEWTON):
        arg = scale_c * rate
        residual = trial_norm - ETA * rate - sigma_a * inverse_sinh(arg)
        slope = -ETA - sigma_a * scale_c / jnp.sqrt(1.0 + arg * arg)
        rate = rate - residual / slope
    return trial_norm, rate


def final_kernel(
    p_in, ain, props, slots,
    v_hbm, rate_out, theta_out,
    sj, xs, ys, jp, v_out, er, sem,
):
    grp = lax.axis_index("grp")
    blk = lax.axis_index("blk")
    lane, sub, jl, k, i_el = tile_iota()

    for dg in (-1, 1):
        both = None
        for db in (-1, 1):
            from_g, from_b = grp + dg, blk + db
            there = (from_g >= 0) & (from_g < N_GRP) & (from_b >= 0) & (from_b < N_BLK)
            at = jnp.where(there, 6 * (from_g * N_BLK + from_b) + 5, 0)
            value = jnp.broadcast_to(ain[pl.ds(at, 1), :], (8, 128))
            value = jnp.where(there, jnp.where(sub % 2 == 0, value, roll(value, -15, 1)), 0.0)
            both = value if both is None else jnp.where(sub < 4, both, value)
        kept = jnp.where((sub < 2) | (sub >= 6), both, 0.0)
        to = 31 if dg > 0 else 0
        for m in range(15):
            er[(dg + 1) // 2, m] = jnp.where(k == to, roll(kept, to - m, 1), 0.0)

    def field(c, p, q, r):
        value = p_in[c, node(p, q, r)]
        if p in (0, 4) and r in (0, 4):
            edge = er[r // 4, c * 5 + q]
            value = value + jnp.where((sub < 4) == (p == 0), edge, 0.0)
        return value

    odd_sub = sub % 2 == 1
    for c in range(3):
        for p in range(5):
            for r in range(5):
                sj[pl.ds(8 * (c * 32 + p * 5 + r), 8), :] = jnp.where(
                    odd_sub, field(c, p, 0, r), field(c, p, 4, r)
                )
        for t in range(25, 32):
            sj[pl.ds(8 * (c * 32 + t), 8), :] = jnp.zeros((8, 128), F32)
    jump = fault_lanes(sj, 96)
    sb = sj
    for i in range(4):
        ys[pl.ds(32 * i, 32), :] = ain[pl.ds(blk // 8 * 192 + i, 32, stride=6), :]
    ys[...] = ys[...].T
    t0x, t0z, scale_c, sigma_a = (ys[pl.ds(25 * j, 32), :] for j in range(4))
    trial_x = t0x + ETA * jump[0:32]
    trial_z = t0z + ETA * jump[64:96]
    trial_norm, rate = solve(trial_x, trial_z, scale_c, sigma_a)
    keep = 1.0 - ETA * rate / jnp.maximum(trial_norm, TRACTION_FLOOR)
    push = (
        CORRECTION * (trial_x * keep - t0x),
        CORRECTION * ETA * jump[32:64],
        CORRECTION * (trial_z * keep - t0z),
    )
    for c in range(3):
        for i in range(4):
            sb[pl.ds(c * 256 + 2 * i + 1, 32, stride=8), :] = roll(push[c], -32 * i, 1)
            sb[pl.ds(c * 256 + 2 * i, 32, stride=8), :] = roll(push[c], 96 - 32 * i, 1)
    plus_at = (sub % 2 == 1) & (lane < 32)
    minus_at = (sub % 2 == 0) & (lane >= 96)
    stores = []
    for c in range(3):
        for p in range(5):
            for r in range(5):
                n0, n4 = node(p, 0, r), node(p, 4, r)
                push_back = sb[pl.ds(8 * (c * 32 + p * 5 + r), 8), :]
                v_out[c, n0, :] = (field(c, p, 0, r) - jnp.where(plus_at, push_back, 0.0)).reshape(1024)
                v_out[c, n4, :] = (field(c, p, 4, r) + jnp.where(minus_at, push_back, 0.0)).reshape(1024)
                for q in (1, 2, 3):
                    v_out[c, node(p, q, r), :] = field(c, p, q, r).reshape(1024)
        stores.append(pltpu.make_async_copy(v_out.at[c], v_hbm.at[c], sem.at[c]))
        stores[c].start()

    for u in range(4):
        heads = ain[pl.ds(u * 192 + grp * 48 + 4, 8, stride=6), :]
        for i in range(4):
            tails = roll(ain[pl.ds(u * 192 + grp * 48 + i, 8, stride=6), :], 60, 1)
            both = jnp.where(lane < 32, roll(heads, -32 * i, 1), tails)
            ys[pl.ds(8 * (u * 4 + i), 8), :] = jnp.where(lane < 60, both, 0.0)
    xs[...] = jnp.zeros((128, 128), F32)
    lane4 = lax.broadcasted_iota(jnp.int32, (4, 128), 1)
    for step, there, i, into in ((-1, grp > 0, 3, 0), (8, grp < N_GRP - 1, 0, 31)):
        first_row = jnp.where(there, (grp * 8 + step) * 6, 0)
        tails = roll(ain[pl.ds(first_row + i, 4, stride=192), :], 60, 1)
        heads = roll(ain[pl.ds(first_row + 4, 4, stride=192), :], -32 * i, 1)
        both = jnp.where(lane4 < 32, heads, tails)
        xs[pl.ds(into, 4, stride=32), :] = jnp.where((lane4 < 60) & there, both, 0.0)
    ys[...] = ys[...].T
    xs[...] = xs[...].T
    first = jnp.where(grp_is(blk, 0), 1.0, 0.0).astype(F32)
    last = jnp.where(grp_is(blk, N_BLK - 1), 1.0, 0.0).astype(F32)

    def along_z(mat, p, c):
        t = mat[pl.ds(6 * (2 * p + c // 2), 8), :]
        low = jnp.where((sub == 0) & (lane >= 32), roll(roll(t, 32, 1), -5, 0), 0.0)
        high = jnp.where((sub == 4) & (lane < 96), roll(roll(t, -32, 1), -1, 0), 0.0)
        return t + low * first + high * last

    i_at, s_at = lane // 8 % 4, lane % 8
    for c in (0, 2):
        t = [along_z(ys, p, c) for p in range(5)]
        end0, end4 = along_z(xs, 0, c), along_z(xs, 4, c)
        left = jnp.where(s_at == 0, end4, roll(t[4], -23, 1))
        right = jnp.where(s_at == 7, end0, roll(t[0], 23, 1))
        t[0], t[4] = (
            t[0] + jnp.where(i_at == 0, left, 0.0),
            t[4] + jnp.where(i_at == 3, right, 0.0),
        )
        for p in range(5):
            jp[c // 2, 5 * p : 5 * p + 5, :] = t[p][0:5]
    hot = slot_hot(slots[...])
    slot_jump = [
        lax.dot_general(
            jp[c], hot, (((1,), (0,)), ((), ())), precision=HIGHEST, preferred_element_type=F32
        )[0:25]
        for c in range(2)
    ]
    theta, a, b, length, pre_x, pre_z, sigma = (props[:, i, :] for i in range(7))
    scale_c = 0.5 * jnp.exp((FRICTION_REF + b * jnp.log(theta / length)) / a)
    _, rate = solve(
        pre_x + ETA * slot_jump[0], pre_z + ETA * slot_jump[1], scale_c, sigma * a
    )
    rate_out[...] = rate
    theta_out[...] = theta + DT * (1.0 - rate * theta / length)
    for copy in stores:
        copy.wait()


def grp_is(index, value):
    return index == value


VMEM_LIMIT = 24 << 20


def shape(*dims):
    return jax.ShapeDtypeStruct(dims, F32)


def vmem(*dims):
    return pltpu.VMEM(dims, F32)


HBM = pl.BlockSpec(memory_space=pltpu.HBM)
WHOLE = pl.BlockSpec(memory_space=pltpu.VMEM)


PARAMS = pltpu.CompilerParams(vmem_limit_bytes=VMEM_LIMIT)
FIELD = (3, 125, 8, 128)


def in_hbm(x):
    return pltpu.with_memory_space_constraint(x, pltpu.HBM)


def force_call(*args):
    return pl.pallas_call(
        force_kernel,
        name="force",
        in_specs=[HBM] * 5,
        out_specs=[WHOLE] * 5 + [HBM],
        out_shape=(
            shape(*FIELD), shape(75, 2, 128), shape(75, 2, 128),
            shape(3, 8, 128), shape(3, 8, 128), pltpu.HBM((768, 128), F32),
        ),
        scratch_shapes=[
            vmem(*FIELD), vmem(*FIELD), vmem(512, 128), vmem(128, 128),
            vmem(3, 125, 1024), vmem(2, 125, 1024), vmem(2, 1024),
            vmem(25, 7, 128), pltpu.VMEM((1, 128), jnp.int32), vmem(768, 128),
            pltpu.SemaphoreType.DMA((8,)), pltpu.SemaphoreType.DMA((4,)),
        ],
        compiler_params=PARAMS,
    )(*[in_hbm(x) for x in args])


def on_device(displacement, velocity, lame, fault_props, fault_slots):
    slots = fault_slots.reshape(1, 128)
    fault_props = jnp.transpose(fault_props, (1, 0, 2))
    even_b = [(i, i ^ 1) for i in range(N_BLK)]
    odd_b = [(i, ((i + 1) ^ 1) - 1) for i in range(1, N_BLK - 1)]
    even_g = [(i, i ^ 1) for i in range(N_GRP)]
    odd_g = [(i, ((i + 1) ^ 1) - 1) for i in range(1, N_GRP - 1)]
    f, xe, xo, ze, zo, abuf = force_call(displacement, velocity, lame, fault_props, slots)
    ain = lax.all_to_all(abuf.reshape(768, 1, 128), ("grp", "blk"), 0, 0, tiled=True)
    ain = ain.reshape(768, 128)
    xe = lax.ppermute(xe, "blk", even_b)
    xo = lax.ppermute(xo, "blk", odd_b)
    ze = lax.ppermute(ze, "grp", even_g)
    zo = lax.ppermute(zo, "grp", odd_g)
    p = pl.pallas_call(
        halo_kernel,
        name="halo",
        in_specs=[WHOLE, HBM] + [WHOLE] * 4,
        out_specs=WHOLE,
        out_shape=shape(*FIELD),
        scratch_shapes=[vmem(3, 125, 1024), pltpu.SemaphoreType.DMA((3,))],
        compiler_params=PARAMS,
    )(f, in_hbm(velocity), xe, xo, ze, zo)
    return pl.pallas_call(
        final_kernel,
        name="final",
        in_specs=[WHOLE] * 4,
        out_specs=[HBM, WHOLE, WHOLE],
        out_shape=(pltpu.HBM((3, 125, 1024), F32), shape(25, 128), shape(25, 128)),
        scratch_shapes=[
            vmem(768, 128), vmem(128, 128), vmem(128, 128), vmem(2, 32, 128),
            vmem(3, 125, 1024), vmem(2, 15, 8, 128), pltpu.SemaphoreType.DMA((3,)),
        ],
        compiler_params=PARAMS,
    )(p, ain, fault_props, slots)


def solution(mesh):
    both = ("grp", "blk")
    return jax.shard_map(
        on_device,
        mesh=mesh,
        in_specs=(P(None, None, both), P(None, None, both), P(None, both), P(None, None, both), P(both)),
        out_specs=(P(None, None, both), P(None, both), P(None, both)),
        check_vma=False,
    )
```

```python
import jax
import jax.numpy as jnp
import numpy as np
from jax import lax
from jax.experimental import pallas as pl
from jax.experimental.pallas import tpu as pltpu
from jax.sharding import PartitionSpec as P

NEWTON = 3
GLL_POINTS = np.array([-1.0, -np.sqrt(3.0 / 7.0), 0.0, np.sqrt(3.0 / 7.0), 1.0])
GLL_WEIGHTS = np.array([0.1, 49.0 / 90.0, 32.0 / 45.0, 49.0 / 90.0, 0.1])
DT = 0.01
W_END = 0.1
ETA = W_END / (2.0 * DT)
CORRECTION = DT / W_END
FRICTION_REF = 0.6
TRACTION_FLOOR = 1.0
N_GRP = 4
N_BLK = 32
F32 = jnp.float32
HIGHEST = lax.Precision.HIGHEST


def derivative_table():
    x = GLL_POINTS
    bary = [1.0 / np.prod([x[c] - x[o] for o in range(5) if o != c]) for c in range(5)]
    table = np.zeros((5, 5))
    for r in range(5):
        for c in range(5):
            if r != c:
                table[r, c] = bary[c] / bary[r] / (x[r] - x[c])
        table[r, r] = -np.sum(table[r])
    return table


D_TABLE = derivative_table()
M_TABLE = -DT * D_TABLE.T * GLL_WEIGHTS[None, :] / GLL_WEIGHTS[:, None]


def line(table, u):
    e0, e1 = u[0] + u[4], u[1] + u[3]
    o0, o1 = u[0] - u[4], u[1] - u[3]
    out = [None] * 5
    for i in range(2):
        even = (
            float((table[i, 0] + table[i, 4]) / 2) * e0
            + float((table[i, 1] + table[i, 3]) / 2) * e1
            + float(table[i, 2]) * u[2]
        )
        odd = (
            float((table[i, 0] - table[i, 4]) / 2) * o0
            + float((table[i, 1] - table[i, 3]) / 2) * o1
        )
        out[i] = odd + even
        out[4 - i] = odd - even
    out[2] = float(table[2, 0]) * o0 + float(table[2, 1]) * o1
    return out


def node(p, q, r):
    return 25 * p + 5 * q + r


def roll(x, shift, axis):
    shift = shift % x.shape[axis]
    return x if shift == 0 else pltpu.roll(x, shift, axis)


def row(ref, c, n):
    return ref[c, n, :].reshape(8, 128)


def tile_iota():
    lane = lax.broadcasted_iota(jnp.int32, (8, 128), 1)
    sub = lax.broadcasted_iota(jnp.int32, (8, 128), 0)
    return lane, sub, lane // 32, lane % 32, sub // 2


def inverse_sinh(value):
    return jnp.log(value + jnp.sqrt(1.0 + value * value))


def own_scales(grp, blk):
    half = lambda has: jnp.where(has, 0.5, 1.0).astype(F32)
    return half(blk > 0), half(blk < N_BLK - 1), half(grp > 0), half(grp < N_GRP - 1)


def slot_hot(slots):
    r = lax.broadcasted_iota(jnp.int32, (128, 128), 0)
    face = (r % 8) * 16 + (r // 8 % 4) * 4 + r // 32
    return (jnp.broadcast_to(slots, (128, 128)) == face).astype(F32)


def fault_lanes(ref, rows):
    block = lax.broadcasted_iota(jnp.int32, (rows, 128), 1) // 32
    plus = [roll(ref[pl.ds(2 * i + 1, rows, stride=8), :], 32 * i, 1) for i in range(4)]
    minus = [roll(ref[pl.ds(2 * i, rows, stride=8), :], 32 * i - 96, 1) for i in range(4)]
    out = plus[0] - minus[0]
    for i in range(1, 4):
        out = jnp.where(block == i, plus[i] - minus[i], out)
    return out


def force_kernel(
    disp_hbm, vel_hbm, lame_hbm, props_hbm, slots_hbm,
    f_out, xe_out, xo_out, ze_out, zo_out, abuf_hbm,
    gx, gy, sj, xs, disp, vel, lame, props, slots, abuf, sem_in, sem_out,
):
    grp = lax.axis_index("grp")
    blk = lax.axis_index("blk")
    pairs = [(disp_hbm.at[0], disp.at[0]), (lame_hbm, lame)]
    pairs += [(disp_hbm.at[1], disp.at[1]), (disp_hbm.at[2], disp.at[2])]
    pairs += [(props_hbm, props), (slots_hbm, slots)]
    pairs += [(vel_hbm.at[0], vel.at[0]), (vel_hbm.at[2], vel.at[1])]
    loads = [pltpu.make_async_copy(a, b, sem_in.at[t]) for t, (a, b) in enumerate(pairs)]
    for load in loads[:6]:
        load.start()
    lane, sub, jl, k, i_el = tile_iota()
    x0, x4, z0, z4 = own_scales(grp, blk)
    xs[...] = jnp.zeros((128, 128), F32)
    abuf[...] = jnp.zeros((768, 128), F32)
    loads[0].wait()

    for c in range(3):
        if c:
            loads[1 + c].wait()
        if c == 2:
            loads[6].start()
            loads[7].start()
        for r in range(5):
            u = [[row(disp, c, node(p, q, r)) for q in range(5)] for p in range(5)]
            for q in range(5):
                out = line(D_TABLE, [u[p][q] for p in range(5)])
                for p in range(5):
                    gx[c, node(p, q, r)] = out[p]
            for p in range(5):
                out = line(D_TABLE, u[p])
                for q in range(5):
                    gy[c, node(p, q, r)] = out[q]

    loads[4].wait()
    loads[5].wait()
    theta, a, b, length, pre_x, pre_z, sigma = (props[:, i, :] for i in range(7))
    xs[0:25] = pre_x
    xs[25:50] = pre_z
    xs[50:75] = 0.5 * jnp.exp((FRICTION_REF + b * jnp.log(theta / length)) / a)
    xs[75:100] = sigma * a
    packed = lax.dot_general(
        slot_hot(slots[...]), xs[...], (((1,), (1,)), ((), ())),
        precision=HIGHEST, preferred_element_type=F32,
    )
    for u in range(4):
        for i in range(4):
            t = u * 4 + i
            abuf[pl.ds(u * 192 + grp * 48 + i, 8, stride=6), :] = packed[8 * t : 8 * t + 8]

    loads[1].wait()
    lam = lame[0, :].reshape(8, 128)
    mu = lame[1, :].reshape(8, 128)
    mu2 = mu + mu
    for p in range(5):
        for q in range(5):
            gz = [
                line(D_TABLE, [row(disp, c, node(p, q, r)) for r in range(5)]) for c in range(3)
            ]
            sz = [[None] * 5 for _ in range(3)]
            for r in range(5):
                n = node(p, q, r)
                g0 = [gx[c, n] for c in range(3)]
                g1 = [gy[c, n] for c in range(3)]
                g2 = [gz[c][r] for c in range(3)]
                spread = lam * (g0[0] + g1[1] + g2[2])
                s01 = mu * (g0[1] + g1[0])
                s02 = mu * (g0[2] + g2[0])
                s12 = mu * (g1[2] + g2[1])
                gx[0, n] = spread + mu2 * g0[0]
                gx[1, n] = s01
                gx[2, n] = s02
                gy[1, n] = spread + mu2 * g1[1]
                gy[2, n] = s12
                sz[0][r], sz[1][r], sz[2][r] = s02, s12, spread + mu2 * g2[2]
            for c in range(3):
                out = line(M_TABLE, sz[c])
                for r in range(5):
                    f_out[c, node(p, q, r)] = out[r]

    y4_in, y0_in = jl < 3, jl > 0
    x4_in, x0_in = i_el < 3, i_el > 0
    z4_in, z0_in = k < 31, k > 0
    zero = jnp.zeros((8, 128), F32)

    def xy_parts(c, r):
        f = [[f_out[c, node(p, q, r)] for q in range(5)] for p in range(5)]
        for p in range(5):
            if c == 0:
                s = [gx[1, node(p, q, r)] for q in range(5)]
            else:
                s = [gy[c, node(p, q, r)] for q in range(5)]
            out = line(M_TABLE, s)
            for q in range(5):
                f[p][q] = f[p][q] + out[q]
        for q in range(5):
            out = line(M_TABLE, [gx[c, node(p, q, r)] for p in range(5)])
            for p in range(5):
                f[p][q] = f[p][q] + out[p]
        for p in range(5):
            up, down = roll(f[p][0], -32, 1), roll(f[p][4], 32, 1)
            f[p][0], f[p][4] = (
                jnp.where(y0_in, 0.5 * (f[p][0] + down), f[p][0]),
                jnp.where(y4_in, 0.5 * (f[p][4] + up), f[p][4]),
            )
        for q in range(5):
            avg = 0.5 * (f[4][q] + roll(f[0][q], -2, 0))
            f[0][q] = jnp.where(x0_in, roll(avg, 2, 0), f[0][q] * x0)
            f[4][q] = jnp.where(x4_in, avg, f[4][q] * x4)
        for p in range(5):
            for q in range(5):
                f_out[c, node(p, q, r)] = f[p][q]

    def assemble(c):
        xy_parts(c, 0)
        xy_parts(c, 4)
        for p in range(5):
            for q in range(5):
                n0, n4 = node(p, q, 0), node(p, q, 4)
                a0, a4 = f_out[c, n0], f_out[c, n4]
                up, down = roll(a0, -1, 1), roll(a4, 1, 1)
                f_out[c, n0] = jnp.where(z0_in, 0.5 * (a0 + down), a0 * z0)
                f_out[c, n4] = jnp.where(z4_in, 0.5 * (a4 + up), a4 * z4)
        for r in (1, 2, 3):
            xy_parts(c, r)

    assemble(0)
    assemble(2)

    loads[6].wait()
    loads[7].wait()
    own_x = {0: jnp.where(x0_in, 1.0, x0), 4: jnp.where(x4_in, 1.0, x4)}
    own_z = {0: jnp.where(z0_in, 1.0, z0), 4: jnp.where(z4_in, 1.0, z4)}
    odd_sub = sub % 2 == 1
    for p in range(5):
        for cc in range(2):
            c = 2 * cc
            at = 6 * (2 * p + cc)
            sides = [None] * 5
            for r in range(5):
                own = None
                for part in (own_x.get(p), own_z.get(r)):
                    if part is not None:
                        own = part if own is None else own * part
                n0, n4 = node(p, 0, r), node(p, 4, r)
                v = jnp.where(odd_sub, row(vel, cc, n0), row(vel, cc, n4))
                f = jnp.where(odd_sub, f_out[c, n0], f_out[c, n4])
                sides[r] = f + (v if own is None else v * own)
                sj[pl.ds(8 * (at + r), 8), :] = sides[r]
            extra = jnp.where(k == 0, roll(sides[4], -31, 1), 0.0)
            extra = jnp.where(k == 31, roll(sides[0], 31, 1), extra)
            sj[pl.ds(8 * (at + 5), 8), :] = extra
    for t in range(60, 64):
        sj[pl.ds(8 * t, 8), :] = zero
    y = fault_lanes(sj, 64)
    yt = jnp.concatenate([y, jnp.zeros((64, 128), F32)]).T
    assemble(1)
    dest = blk // 8
    lane32 = lax.broadcasted_iota(jnp.int32, (32, 128), 1)
    tails = [roll(yt[32 * i : 32 * i + 32], 68, 1) for i in range(4)]
    heads = yt[0:32]
    for i in range(1, 4):
        heads = jnp.where(lane32 // 32 == i, roll(yt[32 * i : 32 * i + 32], 32 * i, 1), heads)

    def put_jump(d):
        for i in range(4):
            rows = pl.ds(d * 192 + i, 32, stride=6)
            abuf[rows, :] = jnp.where(lane32 >= 100, tails[i], abuf[rows, :])
        abuf[pl.ds(d * 192 + 4, 32, stride=6), :] = heads

    put_jump(dest)

    @pl.when((blk % 8 == 7) & (dest < N_GRP - 1))
    def _():
        put_jump(dest + 1)

    @pl.when((blk % 8 == 0) & (dest > 0))
    def _():
        put_jump(dest - 1)

    for dg in (-1, 1):
        edge = zero
        for m in range(15):
            c, q = m // 5, m % 5
            r = 4 if dg > 0 else 0
            value = jnp.where(sub < 4, f_out[c, node(0, q, r)], f_out[c, node(4, q, r)])
            edge = jnp.where(k == m, roll(value, m - (31 if dg > 0 else 0), 1), edge)
        edge = jnp.where(k < 15, edge, roll(roll(edge, 15, 1), -1, 0))
        for db, at in ((-1, 0), (1, 6)):
            to_g, to_b = grp + dg, blk + db
            there = (to_g >= 0) & (to_g < N_GRP) & (to_b >= 0) & (to_b < N_BLK)

            @pl.when(there)
            def _(edge=edge, at=at, to_g=to_g, to_b=to_b):
                abuf[pl.ds(6 * (to_g * N_BLK + to_b) + 5, 1), :] = edge[at : at + 1]

    stores = []
    for t in range(4):
        rows = pl.ds(192 * t, 192)
        stores.append(pltpu.make_async_copy(abuf.at[rows], abuf_hbm.at[rows], sem_out.at[t]))
    for copy in stores:
        copy.start()

    x_even = blk % 2 == 0
    for c in range(3):
        for q in range(5):
            for r in range(5):
                m = c * 25 + q * 5 + r
                lo = f_out[c, node(0, q, r)]
                hi = roll(f_out[c, node(4, q, r)], 2, 0)
                xe_out[m] = jnp.where(x_even, hi, lo)[0:2]
                xo_out[m] = jnp.where(x_even, lo, hi)[0:2]

    z_even = grp % 2 == 0
    for g in range(3):
        zlo = zhi = jnp.zeros((8, 128), F32)
        for m in range(32 * g, min(75, 32 * g + 32)):
            c, pq = m // 25, m % 25
            at = k == m % 32
            zlo = jnp.where(at, roll(f_out[c, 5 * pq], m % 32, 1), zlo)
            zhi = jnp.where(at, roll(f_out[c, 5 * pq + 4], m % 32 - 31, 1), zhi)
        ze_out[g] = jnp.where(z_even, zhi, zlo)
        zo_out[g] = jnp.where(z_even, zlo, zhi)
    for copy in stores:
        copy.wait()


def halo_kernel(f_in, vel_hbm, xe, xo, ze, zo, p_out, vel, sem):
    grp = lax.axis_index("grp")
    blk = lax.axis_index("blk")
    lane, sub, jl, k, i_el = tile_iota()
    loads = [pltpu.make_async_copy(vel_hbm.at[c], vel.at[c], sem.at[c]) for c in range(3)]
    for load in loads:
        load.start()
    x_even = blk % 2 == 0
    z_even = grp % 2 == 0
    zlo = [jnp.where(z_even, zo[g], ze[g]) for g in range(3)]
    zhi = [jnp.where(z_even, ze[g], zo[g]) for g in range(3)]
    for c in range(3):
        loads[c].wait()
        for p in range(5):
            for q in range(5):
                m = c * 25 + p * 5 + q
                add0 = roll(zlo[m // 32], -(m % 32), 1)
                add4 = roll(zhi[m // 32], 31 - m % 32, 1)
                for r in range(5):
                    n = node(p, q, r)
                    value = f_in[c, n] + row(vel, c, n)
                    if r == 0:
                        value = value + jnp.where(k == 0, add0, 0.0)
                    if r == 4:
                        value = value + jnp.where(k == 31, add4, 0.0)
                    p_out[c, n] = value
        for q in range(5):
            for r in range(5):
                m = c * 25 + q * 5 + r
                ev, od = xe[m], xo[m]
                lo, hi = node(0, q, r), node(4, q, r)
                p_out[c, lo, 0:2] = p_out[c, lo, 0:2] + jnp.where(x_even, od, ev)
                p_out[c, hi, 6:8] = p_out[c, hi, 6:8] + jnp.where(x_even, ev, od)


def solve(trial_x, trial_z, scale_c, sigma_a):
    trial_norm = jnp.sqrt(trial_x * trial_x + trial_z * trial_z)
    rate = jnp.zeros_like(trial_norm)
    for _ in range(NEWTON):
        arg = scale_c * rate
        residual = trial_norm - ETA * rate - sigma_a * inverse_sinh(arg)
        slope = -ETA - sigma_a * scale_c / jnp.sqrt(1.0 + arg * arg)
        rate = rate - residual / slope
    return trial_norm, rate


def final_kernel(
    p_in, ain, props_hbm, slots_hbm,
    v_hbm, rate_out, theta_out,
    sj, xs, ys, jp, v_out, er, props, slots, sem, sem_in,
):
    grp = lax.axis_index("grp")
    blk = lax.axis_index("blk")
    pairs = ((props_hbm, props), (slots_hbm, slots))
    loads = [pltpu.make_async_copy(a, b, sem_in.at[t]) for t, (a, b) in enumerate(pairs)]
    for load in loads:
        load.start()
    lane, sub, jl, k, i_el = tile_iota()

    for dg in (-1, 1):
        both = None
        for db in (-1, 1):
            from_g, from_b = grp + dg, blk + db
            there = (from_g >= 0) & (from_g < N_GRP) & (from_b >= 0) & (from_b < N_BLK)
            at = jnp.where(there, 6 * (from_g * N_BLK + from_b) + 5, 0)
            value = jnp.broadcast_to(ain[pl.ds(at, 1), :], (8, 128))
            value = jnp.where(there, jnp.where(sub % 2 == 0, value, roll(value, -15, 1)), 0.0)
            both = value if both is None else jnp.where(sub < 4, both, value)
        kept = jnp.where((sub < 2) | (sub >= 6), both, 0.0)
        to = 31 if dg > 0 else 0
        for m in range(15):
            er[(dg + 1) // 2, m] = jnp.where(k == to, roll(kept, to - m, 1), 0.0)

    def field(c, p, q, r):
        value = p_in[c, node(p, q, r)]
        if p in (0, 4) and r in (0, 4):
            edge = er[r // 4, c * 5 + q]
            value = value + jnp.where((sub < 4) == (p == 0), edge, 0.0)
        return value

    odd_sub = sub % 2 == 1
    for c in range(3):
        for p in range(5):
            for r in range(5):
                sj[pl.ds(8 * (c * 32 + p * 5 + r), 8), :] = jnp.where(
                    odd_sub, field(c, p, 0, r), field(c, p, 4, r)
                )
        for t in range(25, 32):
            sj[pl.ds(8 * (c * 32 + t), 8), :] = jnp.zeros((8, 128), F32)
    jump = fault_lanes(sj, 96)
    sb = sj
    for i in range(4):
        ys[pl.ds(32 * i, 32), :] = ain[pl.ds(blk // 8 * 192 + i, 32, stride=6), :]
    ys[...] = ys[...].T
    t0x, t0z, scale_c, sigma_a = (ys[pl.ds(25 * j, 32), :] for j in range(4))
    trial_x = t0x + ETA * jump[0:32]
    trial_z = t0z + ETA * jump[64:96]
    trial_norm, rate = solve(trial_x, trial_z, scale_c, sigma_a)
    keep = 1.0 - ETA * rate / jnp.maximum(trial_norm, TRACTION_FLOOR)
    push = (
        CORRECTION * (trial_x * keep - t0x),
        CORRECTION * ETA * jump[32:64],
        CORRECTION * (trial_z * keep - t0z),
    )
    for c in range(3):
        for i in range(4):
            sb[pl.ds(c * 256 + 2 * i + 1, 32, stride=8), :] = roll(push[c], -32 * i, 1)
            sb[pl.ds(c * 256 + 2 * i, 32, stride=8), :] = roll(push[c], 96 - 32 * i, 1)
    plus_at = (sub % 2 == 1) & (lane < 32)
    minus_at = (sub % 2 == 0) & (lane >= 96)
    stores = []
    for c in range(3):
        for p in range(5):
            for r in range(5):
                n0, n4 = node(p, 0, r), node(p, 4, r)
                push_back = sb[pl.ds(8 * (c * 32 + p * 5 + r), 8), :]
                v_out[c, n0, :] = (field(c, p, 0, r) - jnp.where(plus_at, push_back, 0.0)).reshape(1024)
                v_out[c, n4, :] = (field(c, p, 4, r) + jnp.where(minus_at, push_back, 0.0)).reshape(1024)
                for q in (1, 2, 3):
                    v_out[c, node(p, q, r), :] = field(c, p, q, r).reshape(1024)
        stores.append(pltpu.make_async_copy(v_out.at[c], v_hbm.at[c], sem.at[c]))
        stores[c].start()

    for u in range(4):
        heads = ain[pl.ds(u * 192 + grp * 48 + 4, 8, stride=6), :]
        for i in range(4):
            tails = roll(ain[pl.ds(u * 192 + grp * 48 + i, 8, stride=6), :], 60, 1)
            both = jnp.where(lane < 32, roll(heads, -32 * i, 1), tails)
            ys[pl.ds(8 * (u * 4 + i), 8), :] = jnp.where(lane < 60, both, 0.0)
    xs[...] = jnp.zeros((128, 128), F32)
    lane4 = lax.broadcasted_iota(jnp.int32, (4, 128), 1)
    for step, there, i, into in ((-1, grp > 0, 3, 0), (8, grp < N_GRP - 1, 0, 31)):
        first_row = jnp.where(there, (grp * 8 + step) * 6, 0)
        tails = roll(ain[pl.ds(first_row + i, 4, stride=192), :], 60, 1)
        heads = roll(ain[pl.ds(first_row + 4, 4, stride=192), :], -32 * i, 1)
        both = jnp.where(lane4 < 32, heads, tails)
        xs[pl.ds(into, 4, stride=32), :] = jnp.where((lane4 < 60) & there, both, 0.0)
    ys[...] = ys[...].T
    xs[...] = xs[...].T
    first = jnp.where(grp_is(blk, 0), 1.0, 0.0).astype(F32)
    last = jnp.where(grp_is(blk, N_BLK - 1), 1.0, 0.0).astype(F32)

    def along_z(mat, p, c):
        t = mat[pl.ds(6 * (2 * p + c // 2), 8), :]
        low = jnp.where((sub == 0) & (lane >= 32), roll(roll(t, 32, 1), -5, 0), 0.0)
        high = jnp.where((sub == 4) & (lane < 96), roll(roll(t, -32, 1), -1, 0), 0.0)
        return t + low * first + high * last

    i_at, s_at = lane // 8 % 4, lane % 8
    for c in (0, 2):
        t = [along_z(ys, p, c) for p in range(5)]
        end0, end4 = along_z(xs, 0, c), along_z(xs, 4, c)
        left = jnp.where(s_at == 0, end4, roll(t[4], -23, 1))
        right = jnp.where(s_at == 7, end0, roll(t[0], 23, 1))
        t[0], t[4] = (
            t[0] + jnp.where(i_at == 0, left, 0.0),
            t[4] + jnp.where(i_at == 3, right, 0.0),
        )
        for p in range(5):
            jp[c // 2, 5 * p : 5 * p + 5, :] = t[p][0:5]
    for load in loads:
        load.wait()
    hot = slot_hot(slots[...])
    slot_jump = [
        lax.dot_general(
            jp[c], hot, (((1,), (0,)), ((), ())), precision=HIGHEST, preferred_element_type=F32
        )[0:25]
        for c in range(2)
    ]
    theta, a, b, length, pre_x, pre_z, sigma = (props[:, i, :] for i in range(7))
    scale_c = 0.5 * jnp.exp((FRICTION_REF + b * jnp.log(theta / length)) / a)
    _, rate = solve(
        pre_x + ETA * slot_jump[0], pre_z + ETA * slot_jump[1], scale_c, sigma * a
    )
    rate_out[...] = rate
    theta_out[...] = theta + DT * (1.0 - rate * theta / length)
    for copy in stores:
        copy.wait()


def grp_is(index, value):
    return index == value


VMEM_LIMIT = 24 << 20


def shape(*dims):
    return jax.ShapeDtypeStruct(dims, F32)


def vmem(*dims):
    return pltpu.VMEM(dims, F32)


HBM = pl.BlockSpec(memory_space=pltpu.HBM)
WHOLE = pl.BlockSpec(memory_space=pltpu.VMEM)


PARAMS = pltpu.CompilerParams(vmem_limit_bytes=VMEM_LIMIT)
FIELD = (3, 125, 8, 128)


def in_hbm(x):
    return pltpu.with_memory_space_constraint(x, pltpu.HBM)


def force_call(*args):
    return pl.pallas_call(
        force_kernel,
        name="force",
        in_specs=[HBM] * 5,
        out_specs=[WHOLE] * 5 + [HBM],
        out_shape=(
            shape(*FIELD), shape(75, 2, 128), shape(75, 2, 128),
            shape(3, 8, 128), shape(3, 8, 128), pltpu.HBM((768, 128), F32),
        ),
        scratch_shapes=[
            vmem(*FIELD), vmem(*FIELD), vmem(512, 128), vmem(128, 128),
            vmem(3, 125, 1024), vmem(2, 125, 1024), vmem(2, 1024),
            vmem(25, 7, 128), pltpu.VMEM((1, 128), jnp.int32), vmem(768, 128),
            pltpu.SemaphoreType.DMA((8,)), pltpu.SemaphoreType.DMA((4,)),
        ],
        compiler_params=PARAMS,
    )(*[in_hbm(x) for x in args])


def on_device(displacement, velocity, lame, fault_props, fault_slots):
    slots = fault_slots.reshape(1, 128)
    fault_props = jnp.transpose(fault_props, (1, 0, 2))
    even_b = [(i, i ^ 1) for i in range(N_BLK)]
    odd_b = [(i, ((i + 1) ^ 1) - 1) for i in range(1, N_BLK - 1)]
    even_g = [(i, i ^ 1) for i in range(N_GRP)]
    odd_g = [(i, ((i + 1) ^ 1) - 1) for i in range(1, N_GRP - 1)]
    f, xe, xo, ze, zo, abuf = force_call(displacement, velocity, lame, fault_props, slots)
    ain = lax.all_to_all(abuf.reshape(768, 1, 128), ("grp", "blk"), 0, 0, tiled=True)
    ain = ain.reshape(768, 128)
    xe = lax.ppermute(xe, "blk", even_b)
    xo = lax.ppermute(xo, "blk", odd_b)
    ze = lax.ppermute(ze, "grp", even_g)
    zo = lax.ppermute(zo, "grp", odd_g)
    p = pl.pallas_call(
        halo_kernel,
        name="halo",
        in_specs=[WHOLE, HBM] + [WHOLE] * 4,
        out_specs=WHOLE,
        out_shape=shape(*FIELD),
        scratch_shapes=[vmem(3, 125, 1024), pltpu.SemaphoreType.DMA((3,))],
        compiler_params=PARAMS,
    )(f, in_hbm(velocity), xe, xo, ze, zo)
    return pl.pallas_call(
        final_kernel,
        name="final",
        in_specs=[WHOLE, WHOLE, HBM, HBM],
        out_specs=[HBM, WHOLE, WHOLE],
        out_shape=(pltpu.HBM((3, 125, 1024), F32), shape(25, 128), shape(25, 128)),
        scratch_shapes=[
            vmem(768, 128), vmem(128, 128), vmem(128, 128), vmem(2, 32, 128),
            vmem(3, 125, 1024), vmem(2, 15, 8, 128), vmem(25, 7, 128),
            pltpu.VMEM((1, 128), jnp.int32), pltpu.SemaphoreType.DMA((3,)),
            pltpu.SemaphoreType.DMA((2,)),
        ],
        compiler_params=PARAMS,
    )(p, ain, in_hbm(fault_props), in_hbm(slots))


def solution(mesh):
    both = ("grp", "blk")
    return jax.shard_map(
        on_device,
        mesh=mesh,
        in_specs=(P(None, None, both), P(None, None, both), P(None, both), P(None, None, both), P(both)),
        out_specs=(P(None, None, both), P(None, both), P(None, both)),
        check_vma=False,
    )
```

```python
import jax
import jax.numpy as jnp
import numpy as np
from jax import lax
from jax.experimental import pallas as pl
from jax.experimental.pallas import tpu as pltpu
from jax.sharding import PartitionSpec as P

NEWTON = 3
GLL_POINTS = np.array([-1.0, -np.sqrt(3.0 / 7.0), 0.0, np.sqrt(3.0 / 7.0), 1.0])
GLL_WEIGHTS = np.array([0.1, 49.0 / 90.0, 32.0 / 45.0, 49.0 / 90.0, 0.1])
DT = 0.01
W_END = 0.1
ETA = W_END / (2.0 * DT)
CORRECTION = DT / W_END
FRICTION_REF = 0.6
TRACTION_FLOOR = 1.0
N_GRP = 4
N_BLK = 32
F32 = jnp.float32
HIGHEST = lax.Precision.HIGHEST


def derivative_table():
    x = GLL_POINTS
    bary = [1.0 / np.prod([x[c] - x[o] for o in range(5) if o != c]) for c in range(5)]
    table = np.zeros((5, 5))
    for r in range(5):
        for c in range(5):
            if r != c:
                table[r, c] = bary[c] / bary[r] / (x[r] - x[c])
        table[r, r] = -np.sum(table[r])
    return table


D_TABLE = derivative_table()
M_TABLE = -DT * D_TABLE.T * GLL_WEIGHTS[None, :] / GLL_WEIGHTS[:, None]


def line(table, u):
    e0, e1 = u[0] + u[4], u[1] + u[3]
    o0, o1 = u[0] - u[4], u[1] - u[3]
    out = [None] * 5
    for i in range(2):
        even = (
            float((table[i, 0] + table[i, 4]) / 2) * e0
            + float((table[i, 1] + table[i, 3]) / 2) * e1
            + float(table[i, 2]) * u[2]
        )
        odd = (
            float((table[i, 0] - table[i, 4]) / 2) * o0
            + float((table[i, 1] - table[i, 3]) / 2) * o1
        )
        out[i] = odd + even
        out[4 - i] = odd - even
    out[2] = float(table[2, 0]) * o0 + float(table[2, 1]) * o1
    return out


def node(p, q, r):
    return 25 * p + 5 * q + r


def roll(x, shift, axis):
    shift = shift % x.shape[axis]
    return x if shift == 0 else pltpu.roll(x, shift, axis)


def row(ref, c, n):
    return ref[c, n, :].reshape(8, 128)


def tile_iota():
    lane = lax.broadcasted_iota(jnp.int32, (8, 128), 1)
    sub = lax.broadcasted_iota(jnp.int32, (8, 128), 0)
    return lane, sub, lane // 32, lane % 32, sub // 2


def inverse_sinh(value):
    return jnp.log(value + jnp.sqrt(1.0 + value * value))


def own_scales(grp, blk):
    half = lambda has: jnp.where(has, 0.5, 1.0).astype(F32)
    return half(blk > 0), half(blk < N_BLK - 1), half(grp > 0), half(grp < N_GRP - 1)


def slot_hot(slots):
    r = lax.broadcasted_iota(jnp.int32, (128, 128), 0)
    face = (r % 8) * 16 + (r // 8 % 4) * 4 + r // 32
    return (jnp.broadcast_to(slots, (128, 128)) == face).astype(F32)


def fault_lanes(ref, rows):
    block = lax.broadcasted_iota(jnp.int32, (rows, 128), 1) // 32
    plus = [roll(ref[pl.ds(2 * i + 1, rows, stride=8), :], 32 * i, 1) for i in range(4)]
    minus = [roll(ref[pl.ds(2 * i, rows, stride=8), :], 32 * i - 96, 1) for i in range(4)]
    out = plus[0] - minus[0]
    for i in range(1, 4):
        out = jnp.where(block == i, plus[i] - minus[i], out)
    return out


def force_kernel(
    disp_hbm, vel_hbm, lame_hbm, props_hbm, slots_hbm,
    f_out, xe_out, xo_out, ze_out, zo_out, abuf_hbm,
    gx, gy, sj, xs, disp, vel, lame, props, slots, abuf, sem_in, sem_out,
):
    grp = lax.axis_index("grp")
    blk = lax.axis_index("blk")
    pairs = [(disp_hbm.at[0], disp.at[0]), (lame_hbm, lame)]
    pairs += [(disp_hbm.at[1], disp.at[1]), (disp_hbm.at[2], disp.at[2])]
    pairs += [(props_hbm, props), (slots_hbm, slots)]
    pairs += [(vel_hbm.at[0], vel.at[0]), (vel_hbm.at[2], vel.at[1])]
    loads = [pltpu.make_async_copy(a, b, sem_in.at[t]) for t, (a, b) in enumerate(pairs)]
    for load in loads[:6]:
        load.start()
    lane, sub, jl, k, i_el = tile_iota()
    x0, x4, z0, z4 = own_scales(grp, blk)
    xs[...] = jnp.zeros((128, 128), F32)
    abuf[...] = jnp.zeros((768, 128), F32)
    loads[0].wait()

    for c in range(3):
        if c:
            loads[1 + c].wait()
        if c == 2:
            loads[6].start()
            loads[7].start()
        for r in range(5):
            u = [[row(disp, c, node(p, q, r)) for q in range(5)] for p in range(5)]
            for q in range(5):
                out = line(D_TABLE, [u[p][q] for p in range(5)])
                for p in range(5):
                    gx[c, node(p, q, r)] = out[p]
            for p in range(5):
                out = line(D_TABLE, u[p])
                for q in range(5):
                    gy[c, node(p, q, r)] = out[q]

    loads[4].wait()
    loads[5].wait()
    theta, a, b, length, pre_x, pre_z, sigma = (props[:, i, :] for i in range(7))
    xs[0:25] = pre_x
    xs[25:50] = pre_z
    xs[50:75] = 0.5 * jnp.exp((FRICTION_REF + b * jnp.log(theta / length)) / a)
    xs[75:100] = sigma * a
    packed = lax.dot_general(
        slot_hot(slots[...]), xs[...], (((1,), (1,)), ((), ())),
        precision=HIGHEST, preferred_element_type=F32,
    )
    for u in range(4):
        for i in range(4):
            t = u * 4 + i
            abuf[pl.ds(u * 192 + grp * 48 + i, 8, stride=6), :] = packed[8 * t : 8 * t + 8]

    loads[1].wait()
    lam = lame[0, :].reshape(8, 128)
    mu = lame[1, :].reshape(8, 128)
    mu2 = mu + mu
    for p in range(5):
        for q in range(5):
            gz = [
                line(D_TABLE, [row(disp, c, node(p, q, r)) for r in range(5)]) for c in range(3)
            ]
            sz = [[None] * 5 for _ in range(3)]
            for r in range(5):
                n = node(p, q, r)
                g0 = [gx[c, n] for c in range(3)]
                g1 = [gy[c, n] for c in range(3)]
                g2 = [gz[c][r] for c in range(3)]
                spread = lam * (g0[0] + g1[1] + g2[2])
                s01 = mu * (g0[1] + g1[0])
                s02 = mu * (g0[2] + g2[0])
                s12 = mu * (g1[2] + g2[1])
                gx[0, n] = spread + mu2 * g0[0]
                gx[1, n] = s01
                gx[2, n] = s02
                gy[1, n] = spread + mu2 * g1[1]
                gy[2, n] = s12
                sz[0][r], sz[1][r], sz[2][r] = s02, s12, spread + mu2 * g2[2]
            for c in range(3):
                out = line(M_TABLE, sz[c])
                for r in range(5):
                    f_out[c, node(p, q, r)] = out[r]

    y4_in, y0_in = jl < 3, jl > 0
    x4_in, x0_in = i_el < 3, i_el > 0
    z4_in, z0_in = k < 31, k > 0
    zero = jnp.zeros((8, 128), F32)

    def xy_parts(c, r):
        f = [[f_out[c, node(p, q, r)] for q in range(5)] for p in range(5)]
        for p in range(5):
            if c == 0:
                s = [gx[1, node(p, q, r)] for q in range(5)]
            else:
                s = [gy[c, node(p, q, r)] for q in range(5)]
            out = line(M_TABLE, s)
            for q in range(5):
                f[p][q] = f[p][q] + out[q]
        for q in range(5):
            out = line(M_TABLE, [gx[c, node(p, q, r)] for p in range(5)])
            for p in range(5):
                f[p][q] = f[p][q] + out[p]
        for p in range(5):
            up, down = roll(f[p][0], -32, 1), roll(f[p][4], 32, 1)
            f[p][0], f[p][4] = (
                jnp.where(y0_in, 0.5 * (f[p][0] + down), f[p][0]),
                jnp.where(y4_in, 0.5 * (f[p][4] + up), f[p][4]),
            )
        for q in range(5):
            avg = 0.5 * (f[4][q] + roll(f[0][q], -2, 0))
            f[0][q] = jnp.where(x0_in, roll(avg, 2, 0), f[0][q] * x0)
            f[4][q] = jnp.where(x4_in, avg, f[4][q] * x4)
        for p in range(5):
            for q in range(5):
                f_out[c, node(p, q, r)] = f[p][q]

    def assemble(c):
        xy_parts(c, 0)
        xy_parts(c, 4)
        for p in range(5):
            for q in range(5):
                n0, n4 = node(p, q, 0), node(p, q, 4)
                a0, a4 = f_out[c, n0], f_out[c, n4]
                up, down = roll(a0, -1, 1), roll(a4, 1, 1)
                f_out[c, n0] = jnp.where(z0_in, 0.5 * (a0 + down), a0 * z0)
                f_out[c, n4] = jnp.where(z4_in, 0.5 * (a4 + up), a4 * z4)
        for r in (1, 2, 3):
            xy_parts(c, r)

    assemble(0)
    assemble(2)

    loads[6].wait()
    loads[7].wait()
    own_x = {0: jnp.where(x0_in, 1.0, x0), 4: jnp.where(x4_in, 1.0, x4)}
    own_z = {0: jnp.where(z0_in, 1.0, z0), 4: jnp.where(z4_in, 1.0, z4)}
    odd_sub = sub % 2 == 1
    for p in range(5):
        for cc in range(2):
            c = 2 * cc
            at = 6 * (2 * p + cc)
            sides = [None] * 5
            for r in range(5):
                own = None
                for part in (own_x.get(p), own_z.get(r)):
                    if part is not None:
                        own = part if own is None else own * part
                n0, n4 = node(p, 0, r), node(p, 4, r)
                v = jnp.where(odd_sub, row(vel, cc, n0), row(vel, cc, n4))
                f = jnp.where(odd_sub, f_out[c, n0], f_out[c, n4])
                sides[r] = f + (v if own is None else v * own)
                sj[pl.ds(8 * (at + r), 8), :] = sides[r]
            extra = jnp.where(k == 0, roll(sides[4], -31, 1), 0.0)
            extra = jnp.where(k == 31, roll(sides[0], 31, 1), extra)
            sj[pl.ds(8 * (at + 5), 8), :] = extra
    for t in range(60, 64):
        sj[pl.ds(8 * t, 8), :] = zero
    y = fault_lanes(sj, 64)
    yt = jnp.concatenate([y, jnp.zeros((64, 128), F32)]).T
    assemble(1)
    for dg in (-1, 1):
        edge = zero
        for m in range(15):
            c, q = m // 5, m % 5
            r = 4 if dg > 0 else 0
            value = jnp.where(sub < 4, f_out[c, node(0, q, r)], f_out[c, node(4, q, r)])
            edge = jnp.where(k == m, roll(value, m - (31 if dg > 0 else 0), 1), edge)
        edge = jnp.where(k < 15, edge, roll(roll(edge, 15, 1), -1, 0))
        for db, at in ((-1, 0), (1, 6)):
            to_g, to_b = grp + dg, blk + db
            there = (to_g >= 0) & (to_g < N_GRP) & (to_b >= 0) & (to_b < N_BLK)

            @pl.when(there)
            def _(edge=edge, at=at, to_g=to_g, to_b=to_b):
                abuf[pl.ds(6 * (to_g * N_BLK + to_b) + 5, 1), :] = edge[at : at + 1]

    dest = blk // 8
    lane32 = lax.broadcasted_iota(jnp.int32, (32, 128), 1)
    tails = [roll(yt[32 * i : 32 * i + 32], 68, 1) for i in range(4)]
    heads = yt[0:32]
    for i in range(1, 4):
        heads = jnp.where(lane32 // 32 == i, roll(yt[32 * i : 32 * i + 32], 32 * i, 1), heads)

    def put_jump(d):
        for i in range(4):
            rows = pl.ds(d * 192 + i, 32, stride=6)
            abuf[rows, :] = jnp.where(lane32 >= 100, tails[i], abuf[rows, :])
        abuf[pl.ds(d * 192 + 4, 32, stride=6), :] = heads

    put_jump(dest)

    @pl.when((blk % 8 == 7) & (dest < N_GRP - 1))
    def _():
        put_jump(dest + 1)

    @pl.when((blk % 8 == 0) & (dest > 0))
    def _():
        put_jump(dest - 1)

    stores = []
    for t in range(4):
        rows = pl.ds(192 * t, 192)
        stores.append(pltpu.make_async_copy(abuf.at[rows], abuf_hbm.at[rows], sem_out.at[t]))
    for copy in stores:
        copy.start()

    x_even = blk % 2 == 0
    for c in range(3):
        for q in range(5):
            for r in range(5):
                m = c * 25 + q * 5 + r
                lo = f_out[c, node(0, q, r)]
                hi = roll(f_out[c, node(4, q, r)], 2, 0)
                xe_out[m] = jnp.where(x_even, hi, lo)[0:2]
                xo_out[m] = jnp.where(x_even, lo, hi)[0:2]

    z_even = grp % 2 == 0
    for g in range(3):
        zlo = zhi = jnp.zeros((8, 128), F32)
        for m in range(32 * g, min(75, 32 * g + 32)):
            c, pq = m // 25, m % 25
            at = k == m % 32
            zlo = jnp.where(at, roll(f_out[c, 5 * pq], m % 32, 1), zlo)
            zhi = jnp.where(at, roll(f_out[c, 5 * pq + 4], m % 32 - 31, 1), zhi)
        ze_out[g] = jnp.where(z_even, zhi, zlo)
        zo_out[g] = jnp.where(z_even, zlo, zhi)
    for copy in stores:
        copy.wait()


def halo_kernel(f_in, vel_hbm, xe, xo, ze, zo, p_out, vel, sem):
    grp = lax.axis_index("grp")
    blk = lax.axis_index("blk")
    lane, sub, jl, k, i_el = tile_iota()
    loads = [pltpu.make_async_copy(vel_hbm.at[c], vel.at[c], sem.at[c]) for c in range(3)]
    for load in loads:
        load.start()
    x_even = blk % 2 == 0
    z_even = grp % 2 == 0
    zlo = [jnp.where(z_even, zo[g], ze[g]) for g in range(3)]
    zhi = [jnp.where(z_even, ze[g], zo[g]) for g in range(3)]
    for c in range(3):
        loads[c].wait()
        for p in range(5):
            for q in range(5):
                m = c * 25 + p * 5 + q
                add0 = roll(zlo[m // 32], -(m % 32), 1)
                add4 = roll(zhi[m // 32], 31 - m % 32, 1)
                for r in range(5):
                    n = node(p, q, r)
                    value = f_in[c, n] + row(vel, c, n)
                    if r == 0:
                        value = value + jnp.where(k == 0, add0, 0.0)
                    if r == 4:
                        value = value + jnp.where(k == 31, add4, 0.0)
                    p_out[c, n] = value
        for q in range(5):
            for r in range(5):
                m = c * 25 + q * 5 + r
                ev, od = xe[m], xo[m]
                lo, hi = node(0, q, r), node(4, q, r)
                p_out[c, lo, 0:2] = p_out[c, lo, 0:2] + jnp.where(x_even, od, ev)
                p_out[c, hi, 6:8] = p_out[c, hi, 6:8] + jnp.where(x_even, ev, od)


def solve(trial_x, trial_z, scale_c, sigma_a):
    trial_norm = jnp.sqrt(trial_x * trial_x + trial_z * trial_z)
    rate = jnp.zeros_like(trial_norm)
    for _ in range(NEWTON):
        arg = scale_c * rate
        residual = trial_norm - ETA * rate - sigma_a * inverse_sinh(arg)
        slope = -ETA - sigma_a * scale_c / jnp.sqrt(1.0 + arg * arg)
        rate = rate - residual / slope
    return trial_norm, rate


def final_kernel(
    p_in, ain, props_hbm, slots_hbm,
    v_hbm, rate_out, theta_out,
    sj, xs, ys, jp, v_out, er, props, slots, sem, sem_in,
):
    grp = lax.axis_index("grp")
    blk = lax.axis_index("blk")
    pairs = ((props_hbm, props), (slots_hbm, slots))
    loads = [pltpu.make_async_copy(a, b, sem_in.at[t]) for t, (a, b) in enumerate(pairs)]
    for load in loads:
        load.start()
    lane, sub, jl, k, i_el = tile_iota()

    for dg in (-1, 1):
        both = None
        for db in (-1, 1):
            from_g, from_b = grp + dg, blk + db
            there = (from_g >= 0) & (from_g < N_GRP) & (from_b >= 0) & (from_b < N_BLK)
            at = jnp.where(there, 6 * (from_g * N_BLK + from_b) + 5, 0)
            value = jnp.broadcast_to(ain[pl.ds(at, 1), :], (8, 128))
            value = jnp.where(there, jnp.where(sub % 2 == 0, value, roll(value, -15, 1)), 0.0)
            both = value if both is None else jnp.where(sub < 4, both, value)
        kept = jnp.where((sub < 2) | (sub >= 6), both, 0.0)
        to = 31 if dg > 0 else 0
        for m in range(15):
            er[(dg + 1) // 2, m] = jnp.where(k == to, roll(kept, to - m, 1), 0.0)

    def field(c, p, q, r):
        value = p_in[c, node(p, q, r)]
        if p in (0, 4) and r in (0, 4):
            edge = er[r // 4, c * 5 + q]
            value = value + jnp.where((sub < 4) == (p == 0), edge, 0.0)
        return value

    odd_sub = sub % 2 == 1
    for c in range(3):
        for p in range(5):
            for r in range(5):
                sj[pl.ds(8 * (c * 32 + p * 5 + r), 8), :] = jnp.where(
                    odd_sub, field(c, p, 0, r), field(c, p, 4, r)
                )
        for t in range(25, 32):
            sj[pl.ds(8 * (c * 32 + t), 8), :] = jnp.zeros((8, 128), F32)
    jump = fault_lanes(sj, 96)
    sb = sj
    for i in range(4):
        ys[pl.ds(32 * i, 32), :] = ain[pl.ds(blk // 8 * 192 + i, 32, stride=6), :]
    ys[...] = ys[...].T
    t0x, t0z, scale_c, sigma_a = (ys[pl.ds(25 * j, 32), :] for j in range(4))
    trial_x = t0x + ETA * jump[0:32]
    trial_z = t0z + ETA * jump[64:96]
    trial_norm, rate = solve(trial_x, trial_z, scale_c, sigma_a)
    keep = 1.0 - ETA * rate / jnp.maximum(trial_norm, TRACTION_FLOOR)
    push = (
        CORRECTION * (trial_x * keep - t0x),
        CORRECTION * ETA * jump[32:64],
        CORRECTION * (trial_z * keep - t0z),
    )
    for c in range(3):
        for i in range(4):
            sb[pl.ds(c * 256 + 2 * i + 1, 32, stride=8), :] = roll(push[c], -32 * i, 1)
            sb[pl.ds(c * 256 + 2 * i, 32, stride=8), :] = roll(push[c], 96 - 32 * i, 1)
    plus_at = (sub % 2 == 1) & (lane < 32)
    minus_at = (sub % 2 == 0) & (lane >= 96)
    stores = []
    for c in range(3):
        for p in range(5):
            for r in range(5):
                n0, n4 = node(p, 0, r), node(p, 4, r)
                push_back = sb[pl.ds(8 * (c * 32 + p * 5 + r), 8), :]
                v_out[c, n0, :] = (field(c, p, 0, r) - jnp.where(plus_at, push_back, 0.0)).reshape(1024)
                v_out[c, n4, :] = (field(c, p, 4, r) + jnp.where(minus_at, push_back, 0.0)).reshape(1024)
                for q in (1, 2, 3):
                    v_out[c, node(p, q, r), :] = field(c, p, q, r).reshape(1024)
        stores.append(pltpu.make_async_copy(v_out.at[c], v_hbm.at[c], sem.at[c]))
        stores[c].start()

    for u in range(4):
        heads = ain[pl.ds(u * 192 + grp * 48 + 4, 8, stride=6), :]
        for i in range(4):
            tails = roll(ain[pl.ds(u * 192 + grp * 48 + i, 8, stride=6), :], 60, 1)
            both = jnp.where(lane < 32, roll(heads, -32 * i, 1), tails)
            ys[pl.ds(8 * (u * 4 + i), 8), :] = jnp.where(lane < 60, both, 0.0)
    xs[...] = jnp.zeros((128, 128), F32)
    lane4 = lax.broadcasted_iota(jnp.int32, (4, 128), 1)
    for step, there, i, into in ((-1, grp > 0, 3, 0), (8, grp < N_GRP - 1, 0, 31)):
        first_row = jnp.where(there, (grp * 8 + step) * 6, 0)
        tails = roll(ain[pl.ds(first_row + i, 4, stride=192), :], 60, 1)
        heads = roll(ain[pl.ds(first_row + 4, 4, stride=192), :], -32 * i, 1)
        both = jnp.where(lane4 < 32, heads, tails)
        xs[pl.ds(into, 4, stride=32), :] = jnp.where((lane4 < 60) & there, both, 0.0)
    ys[...] = ys[...].T
    xs[...] = xs[...].T
    first = jnp.where(grp_is(blk, 0), 1.0, 0.0).astype(F32)
    last = jnp.where(grp_is(blk, N_BLK - 1), 1.0, 0.0).astype(F32)

    def along_z(mat, p, c):
        t = mat[pl.ds(6 * (2 * p + c // 2), 8), :]
        low = jnp.where((sub == 0) & (lane >= 32), roll(roll(t, 32, 1), -5, 0), 0.0)
        high = jnp.where((sub == 4) & (lane < 96), roll(roll(t, -32, 1), -1, 0), 0.0)
        return t + low * first + high * last

    i_at, s_at = lane // 8 % 4, lane % 8
    for c in (0, 2):
        t = [along_z(ys, p, c) for p in range(5)]
        end0, end4 = along_z(xs, 0, c), along_z(xs, 4, c)
        left = jnp.where(s_at == 0, end4, roll(t[4], -23, 1))
        right = jnp.where(s_at == 7, end0, roll(t[0], 23, 1))
        t[0], t[4] = (
            t[0] + jnp.where(i_at == 0, left, 0.0),
            t[4] + jnp.where(i_at == 3, right, 0.0),
        )
        for p in range(5):
            jp[c // 2, 5 * p : 5 * p + 5, :] = t[p][0:5]
    for load in loads:
        load.wait()
    hot = slot_hot(slots[...])
    slot_jump = [
        lax.dot_general(
            jp[c], hot, (((1,), (0,)), ((), ())), precision=HIGHEST, preferred_element_type=F32
        )[0:25]
        for c in range(2)
    ]
    theta, a, b, length, pre_x, pre_z, sigma = (props[:, i, :] for i in range(7))
    scale_c = 0.5 * jnp.exp((FRICTION_REF + b * jnp.log(theta / length)) / a)
    _, rate = solve(
        pre_x + ETA * slot_jump[0], pre_z + ETA * slot_jump[1], scale_c, sigma * a
    )
    rate_out[...] = rate
    theta_out[...] = theta + DT * (1.0 - rate * theta / length)
    for copy in stores:
        copy.wait()


def grp_is(index, value):
    return index == value


VMEM_LIMIT = 24 << 20


def shape(*dims):
    return jax.ShapeDtypeStruct(dims, F32)


def vmem(*dims):
    return pltpu.VMEM(dims, F32)


HBM = pl.BlockSpec(memory_space=pltpu.HBM)
WHOLE = pl.BlockSpec(memory_space=pltpu.VMEM)


PARAMS = pltpu.CompilerParams(vmem_limit_bytes=VMEM_LIMIT)
FIELD = (3, 125, 8, 128)


def in_hbm(x):
    return pltpu.with_memory_space_constraint(x, pltpu.HBM)


def force_call(*args):
    return pl.pallas_call(
        force_kernel,
        name="force",
        in_specs=[HBM] * 5,
        out_specs=[WHOLE] * 5 + [HBM],
        out_shape=(
            shape(*FIELD), shape(75, 2, 128), shape(75, 2, 128),
            shape(3, 8, 128), shape(3, 8, 128), pltpu.HBM((768, 128), F32),
        ),
        scratch_shapes=[
            vmem(*FIELD), vmem(*FIELD), vmem(512, 128), vmem(128, 128),
            vmem(3, 125, 1024), vmem(2, 125, 1024), vmem(2, 1024),
            vmem(25, 7, 128), pltpu.VMEM((1, 128), jnp.int32), vmem(768, 128),
            pltpu.SemaphoreType.DMA((8,)), pltpu.SemaphoreType.DMA((4,)),
        ],
        compiler_params=PARAMS,
    )(*[in_hbm(x) for x in args])


def on_device(displacement, velocity, lame, fault_props, fault_slots):
    slots = fault_slots.reshape(1, 128)
    fault_props = jnp.transpose(fault_props, (1, 0, 2))
    even_b = [(i, i ^ 1) for i in range(N_BLK)]
    odd_b = [(i, ((i + 1) ^ 1) - 1) for i in range(1, N_BLK - 1)]
    even_g = [(i, i ^ 1) for i in range(N_GRP)]
    odd_g = [(i, ((i + 1) ^ 1) - 1) for i in range(1, N_GRP - 1)]
    f, xe, xo, ze, zo, abuf = force_call(displacement, velocity, lame, fault_props, slots)
    ain = lax.all_to_all(abuf.reshape(768, 1, 128), ("grp", "blk"), 0, 0, tiled=True)
    ain = ain.reshape(768, 128)
    xe = lax.ppermute(xe, "blk", even_b)
    xo = lax.ppermute(xo, "blk", odd_b)
    ze = lax.ppermute(ze, "grp", even_g)
    zo = lax.ppermute(zo, "grp", odd_g)
    p = pl.pallas_call(
        halo_kernel,
        name="halo",
        in_specs=[WHOLE, HBM] + [WHOLE] * 4,
        out_specs=WHOLE,
        out_shape=shape(*FIELD),
        scratch_shapes=[vmem(3, 125, 1024), pltpu.SemaphoreType.DMA((3,))],
        compiler_params=PARAMS,
    )(f, in_hbm(velocity), xe, xo, ze, zo)
    return pl.pallas_call(
        final_kernel,
        name="final",
        in_specs=[WHOLE, WHOLE, HBM, HBM],
        out_specs=[HBM, WHOLE, WHOLE],
        out_shape=(pltpu.HBM((3, 125, 1024), F32), shape(25, 128), shape(25, 128)),
        scratch_shapes=[
            vmem(768, 128), vmem(128, 128), vmem(128, 128), vmem(2, 32, 128),
            vmem(3, 125, 1024), vmem(2, 15, 8, 128), vmem(25, 7, 128),
            pltpu.VMEM((1, 128), jnp.int32), pltpu.SemaphoreType.DMA((3,)),
            pltpu.SemaphoreType.DMA((2,)),
        ],
        compiler_params=PARAMS,
    )(p, ain, in_hbm(fault_props), in_hbm(slots))


def solution(mesh):
    both = ("grp", "blk")
    return jax.shard_map(
        on_device,
        mesh=mesh,
        in_specs=(P(None, None, both), P(None, None, both), P(None, both), P(None, None, both), P(both)),
        out_specs=(P(None, None, both), P(None, both), P(None, both)),
        check_vma=False,
    )
```
